32 devices in a mesh: row: 8 (over y, x, core), col: 4 (over z).
Axes of the slice: x: 2, y: 2, z: 4, core: 2. Of those that a mesh axis runs over, the one named last changes fastest.
Arguments:
- x_mat: float32 [512, 512], replicated, may hold values from -8 to 40, as said below
- y_inv: float32 [512, 512], replicated, may hold values from -8 to 40, as said below
- panel_blocks: bfloat16 [512, 4096], replicated, may hold values from -6 to 6
- panel_pos: int32 [512], replicated, may hold values from 0 to 63
- group_blocks: int32 [32, 2], replicated, may hold values from 0 to 63
- cons_blocks: bfloat16 [57344, 4096], P(('row', 'col')), may hold values from -6 to 6
- slot_block: int32 [57344], P(('row', 'col')), may hold values from 0 to 1
- slot_row: int32 [57344], P(('row', 'col')), may hold values from 0 to 32767, as said below
- group_size: int32 [32], P(('row', 'col')), may hold values from 768 to 1792, as said below
- trailing: float32 [32768, 2048], P('row', 'col'), may hold values from -6 to 6
Outputs:
- lower_panel: float32 [32768, 512], P(('row', 'col'))
- updated: float32 [32768, 2048], P('row', 'col')
The draws below stay inside these ranges and needn't reach their ends.
Inputs may be any that keep to these rules, and one draw needn't show every extreme that they name: `x_mat`: symmetric positive definite. `y_inv`: symmetric positive definite. `slot_row`: over all groups, the live slots hold every row 0 to 32767 exactly once; the live slots of one group hold at most 56 rows of one aligned range of 1024 rows, and that most is reached in every draw; other slots hold arbitrary rows. `group_size`: the live slots of a group are its first slots; some group has exactly 1792 in every draw.
All inputs are finite; a program needn't handle non-finite values.
Results may differ from the reference program's by a relative error of at most 0.004.
Values may be sent and summed in bfloat16 or wider, within the bound.
A program may use at most 192 MiB of HBM per device.

```python
import math
import jax
import jax.numpy as jnp
from jax import lax

N = 512
BS = 64
NB = 8
PANEL = 512
TRAIL = 2048
CAP = 2
ROWS_DEV = 4096
M2 = 32768
SUB = 1024
CS = 1792
RB = 64
N_ROW = 8
N_COL = 4
DEVICES = 32


def spd_matrix(key, salt):
    key_one = jax.random.fold_in(jax.random.fold_in(key, salt), 0)
    base = jax.random.normal(key_one, (N, N), jnp.float32)
    gram = jnp.dot(base, base.T, precision=lax.Precision.HIGHEST) / N
    return gram + 0.3 * jnp.eye(N, dtype=jnp.float32)


def draw_x_mat(key, part):
    return spd_matrix(key, 3)


def draw_y_inv(key, part):
    return spd_matrix(key, 5)


def slot_layout(key):
    devices = N_ROW * N_COL
    base_share = SUB // devices
    spread = SUB - devices // 4 * base_share
    key_list = jax.random.split(jax.random.fold_in(key, 11), 5)
    heavy_part = jax.random.permutation(key_list[0], jnp.where(jnp.arange(devices) < devices // 4, base_share, 0).astype(jnp.int32))
    extra_part = jax.random.permutation(key_list[1], (spread // devices + (jnp.arange(devices) < spread % devices).astype(jnp.int32)).astype(jnp.int32))
    source_ids = jnp.arange(devices)[:, None]
    dest_ids = jnp.arange(devices)[None, :]
    counts = heavy_part[:, None] + extra_part[(source_ids + dest_ids) % devices]
    recv_start = jnp.cumsum(counts, axis=0) - counts
    orders = jax.vmap(lambda sub_key: jax.random.permutation(sub_key, SUB))(jax.random.split(key_list[2], devices))
    send_end = jnp.cumsum(counts, axis=1)
    send_start = send_end - counts
    group_total = send_end[:, -1]
    slot_ids = jnp.arange(CS, dtype=jnp.int32)
    dest_of = jax.vmap(lambda ends: jnp.searchsorted(ends, slot_ids, side='right'))(send_end)
    dest_clip = jnp.minimum(dest_of, devices - 1).astype(jnp.int32)
    offset = slot_ids[None, :] - jnp.take_along_axis(send_start, dest_clip, axis=1)
    local_pos = jnp.clip(jnp.take_along_axis(recv_start, dest_clip, axis=1) + offset, 0, SUB - 1)
    local_row = orders[dest_clip, local_pos]
    live_slots = slot_ids[None, :] < group_total[:, None]
    dead_rows = jax.random.randint(key_list[3], (devices, CS), 0, M2)
    row_ids = jnp.where(live_slots, dest_clip * SUB + local_row, dead_rows)
    sort_key = jax.random.randint(key_list[4], (devices, CS), 0, 1 << 20) + jnp.where(live_slots, 0, 1 << 21)
    shuffle = jnp.argsort(sort_key, axis=1, stable=True)
    row_ids = jnp.take_along_axis(row_ids, shuffle, axis=1)
    return (row_ids.reshape(-1).astype(jnp.int32), group_total.astype(jnp.int32))


def draw_slot_row(key, part):
    return slot_layout(key)[0]


def draw_group_size(key, part):
    return slot_layout(key)[1]


def set_ends(result, rng, smallest, high):
    dims = result.shape
    place = [jax.random.randint(jax.random.fold_in(rng, axis), (), 0, dims[axis]) for axis in range(len(dims))]
    result = result.at[tuple(place)].set(smallest)
    longest = dims.index(max(dims))
    place[longest] = (place[longest] + 1) % dims[longest]
    return result.at[tuple(place)].set(high)


def block_levels(own_key, extent, cuts, smallest, high):
    def one(dim, blocks):
        heights = jax.random.uniform(jax.random.fold_in(jax.random.fold_in(own_key, 6), dim), (blocks,), jnp.float32, smallest / len(cuts), high / len(cuts))
        return jnp.repeat(jnp.exp(heights), extent[dim] // blocks).reshape((-1,) + (1,) * (len(extent) - dim - 1))

    loudness = one(*cuts[0])
    for cut in cuts[1:]:
        loudness = loudness * one(*cut)
    return loudness


def normal_values(key, shape, scale, bound, cuts=(), kind=jnp.bfloat16):
    result = jax.random.normal(key, shape, jnp.float32) * scale
    if len(cuts) > 0:
        result = block_levels(key, shape, cuts, -0.22, 0.18) * result
    return jnp.clip(result, min=-bound, max=bound).astype(kind)


def setup_inputs(seed: int = 0) -> dict:
    seeds = jax.random.split(jax.random.key(seed), 11)
    return {
        "x_mat": draw_x_mat(jax.random.fold_in(seeds[10], 71), 0),
        "y_inv": draw_y_inv(jax.random.fold_in(seeds[10], 71), 0),
        "panel_blocks": normal_values(seeds[2], (PANEL, BS * BS), 1.0, 6.0),
        "panel_pos": set_ends(jax.random.randint(seeds[3], (PANEL,), 0, NB * NB), jax.random.fold_in(seeds[3], 1), 0, (NB * NB) - 1).astype(jnp.int32),
        "group_blocks": set_ends(jax.random.randint(seeds[4], (DEVICES, CAP), 0, NB * NB), jax.random.fold_in(seeds[4], 1), 0, (NB * NB) - 1).astype(jnp.int32),
        "cons_blocks": normal_values(seeds[5], (DEVICES * CS, BS * BS), 1.0, 6.0, ((0, 32),)),
        "slot_block": set_ends(jax.random.randint(seeds[6], (DEVICES * CS,), 0, CAP), jax.random.fold_in(seeds[6], 1), 0, CAP - 1).astype(jnp.int32),
        "slot_row": draw_slot_row(jax.random.fold_in(seeds[10], 71), 0),
        "group_size": draw_group_size(jax.random.fold_in(seeds[10], 71), 0),
        "trailing": normal_values(seeds[9], (M2, TRAIL), 1.0, 6.0, ((0, 8), (1, 4)), jnp.float32),
    }


def build_h(values, position, x_mat, y_inv):
    highest = lax.Precision.HIGHEST
    matrix_order = x_mat.shape[0]
    block_size = math.isqrt(values.shape[0])
    block_count = matrix_order // block_size
    e_mat = values.reshape(block_size, block_size).astype(jnp.float32)
    row_start = position // block_count * block_size
    col_start = position % block_count * block_size
    x_left = lax.dynamic_slice_in_dim(x_mat, row_start, block_size, 1)
    x_right = lax.dynamic_slice_in_dim(x_mat, col_start, block_size, 1)
    y_low = lax.dynamic_slice_in_dim(y_inv, col_start, block_size, 0)
    y_high = lax.dynamic_slice_in_dim(y_inv, row_start, block_size, 0)
    term_one = jnp.dot(jnp.dot(x_left, e_mat, precision=highest), y_low, precision=highest)
    term_two = jnp.dot(jnp.dot(x_right, e_mat.T, precision=highest), y_high, precision=highest)
    g_mat = term_one + term_two
    h_mat = (g_mat + g_mat.T).astype(jnp.bfloat16)
    h_mat = h_mat.reshape(block_count, block_size, block_count, block_size).transpose(0, 2, 1, 3)
    return h_mat.reshape(block_count * block_count, block_size * block_size)

def reference(x_mat, y_inv, panel_blocks, panel_pos, group_blocks, cons_blocks, slot_block, slot_row, group_size, trailing):
    highest = lax.Precision.HIGHEST
    devices = N_ROW * N_COL
    blocks_all = lax.map(lambda pair_item: build_h(pair_item[0], pair_item[1], x_mat, y_inv), (panel_blocks, panel_pos))
    panel_float = panel_blocks.astype(jnp.float32)

    def diag_column(blocks_one):
        chosen = jnp.take(blocks_one, panel_pos, axis=0).astype(jnp.float32)
        return lax.optimization_barrier(jnp.sum(panel_float * chosen, axis=1))
    panel_schur = lax.map(diag_column, blocks_all).T
    symmetric = 0.5 * (panel_schur + panel_schur.T)
    diag_shift = 0.01 * jnp.mean(jnp.diagonal(symmetric))
    factor = jnp.linalg.cholesky(symmetric + diag_shift * jnp.eye(PANEL, dtype=jnp.float32))

    def device_rows(dev_item):
        cons_dev, blocks_dev, which_dev = dev_item
        cons_float = cons_dev.astype(jnp.float32)
        running = jnp.zeros((CS, PANEL), jnp.float32)
        for slot_index in range(CAP):
            table = jnp.take(blocks_all, blocks_dev[slot_index], axis=1).astype(jnp.float32)
            product_part = jnp.dot(cons_float, table.T, precision=highest)
            running = jnp.where((which_dev == slot_index)[:, None], product_part, running)
        return running
    rows_all = lax.map(device_rows, (cons_blocks.reshape(devices, CS, BS * BS), group_blocks, slot_block.reshape(devices, CS)))
    live_slots = jnp.arange(CS, dtype=jnp.int32)[None, :] < group_size[:, None]
    target = jnp.where(live_slots, slot_row.reshape(devices, CS), M2).astype(jnp.int32)
    row_schur = jnp.zeros((M2, PANEL), jnp.float32).at[target.reshape(-1)].set(rows_all.reshape(-1, PANEL), mode='drop')
    lower_panel = lax.linalg.triangular_solve(factor, row_schur, left_side=False, lower=True, transpose_a=True)
    col_ids = jnp.arange(TRAIL, dtype=jnp.int32)
    source = col_ids // RB % N_ROW * ROWS_DEV + col_ids // (RB * N_ROW) * RB + col_ids % RB
    picked = jnp.take(lower_panel, source.astype(jnp.int32), axis=0)
    updated = trailing - jnp.dot(lower_panel, picked.T, precision=highest)
    return (lower_panel, updated)
```

```python
import functools
import math

import jax
import jax.numpy as jnp
from jax import lax
from jax.experimental import pallas as pl
from jax.experimental.pallas import tpu as pltpu
from jax.sharding import PartitionSpec as P

BF16 = jnp.bfloat16
F32 = jnp.float32


def split(value):
    high = value.astype(BF16)
    low = (value - high.astype(F32)).astype(BF16)
    return high, low

def lane_half(rows, width):
    return lax.broadcasted_iota(jnp.int32, (rows, width), 1) < width // 2

def unpack_pairs(panel_ref, pairs, count, block_size):
    lanes = 2 * block_size
    keep = lane_half(count, lanes)
    for c in range(block_size // 2):
        both = panel_ref[:, c * lanes : (c + 1) * lanes].astype(F32)
        turned = pltpu.roll(both, block_size, 1)
        pitch = block_size + 1
        pairs[pl.ds(2 * c, count, stride=pitch), :] = jnp.where(keep, both, turned)
        pairs[pl.ds(2 * c + 1, count, stride=pitch), :] = jnp.where(keep, turned, both)

def column_block(ref, block, slot, block_size):
    lanes = 2 * block_size
    start = pl.multiple_of(block // 2 * lanes, lanes)
    wide = ref[:, pl.ds(start, lanes)]
    return jnp.where(block % 2 == slot, wide, pltpu.roll(wide, block_size, 1))

def group_kernel(block_count, tile, pos_ref, own_ref, x_ref, y_ref, panel_ref, out_ref, left, right, pairs, scr, mid):
    step = pl.program_id(0)
    order = x_ref.shape[0]
    block_size = order // block_count
    lanes = 2 * block_size
    half = lane_half(order, lanes)

    @pl.when(step == 0)
    def _():
        for s in range(2):
            position = own_ref[s]
            a = pl.multiple_of(position // block_count * block_size, block_size)
            xa = x_ref[pl.ds(a, block_size), :]
            ya = y_ref[pl.ds(a, block_size), :]
            for p in range(block_count):
                cols = slice(p * block_size, (p + 1) * block_size)
                high, low = split(jnp.concatenate([xa[:, cols], ya[:, cols]], axis=1))
                left[p, s * block_size : (s + 1) * block_size, :] = high
                left[p, (2 + s) * block_size : (3 + s) * block_size, :] = low
        for m, ref in enumerate((y_ref, x_ref)):
            first = column_block(ref, own_ref[0] % block_count, 0, block_size)
            second = column_block(ref, own_ref[1] % block_count, 1, block_size)
            high, low = split(jnp.where(half, first, second))
            for q in range(block_count):
                rows = slice(q * block_size, (q + 1) * block_size)
                cols = slice(m * lanes, (m + 1) * lanes)
                right[q, :block_size, cols] = high[rows]
                right[q, block_size:, cols] = low[rows]

    unpack_pairs(panel_ref, pairs, tile, block_size)
    keep = lane_half(block_size, lanes)
    dot = functools.partial(jnp.dot, preferred_element_type=F32)

    def spread(j, e, t):
        position = pos_ref[step * tile + j]
        p = position // block_count
        q = position % block_count
        top = dot(e, right[q])
        low_part = dot(t, right[p])
        for m, part in enumerate((top[:, :lanes], top[:, lanes:], low_part[:, :lanes], low_part[:, lanes:])):
            high, low = split(part)
            rows = slice(m * block_size, (m + 1) * block_size)
            mid[j, rows, :lanes] = high
            mid[j, rows, lanes:] = low

    def two(i, carry):
        pitch = block_size + 1
        block = jnp.concatenate(
            [pairs[pl.ds(2 * i * pitch, block_size), :], pairs[pl.ds((2 * i + 1) * pitch, block_size), :]],
            axis=0,
        )
        turned = block.T[:block_size]
        swapped = pltpu.roll(turned, block_size, 1)
        e = block.astype(BF16)
        spread(2 * i, e[:block_size], jnp.where(keep, turned, swapped).astype(BF16))
        spread(2 * i + 1, e[block_size:], jnp.where(keep, swapped, turned).astype(BF16))
        return carry

    lax.fori_loop(0, tile // 2, two, 0, unroll=tile // 2)

    def collect(j, carry):
        position = pos_ref[step * tile + j]
        a = jnp.concatenate([left[position // block_count], left[position % block_count]], axis=1)
        h = dot(a, mid[j])
        b = block_size
        quad = lambda r, c: jnp.where(
            keep, h[r : r + b, c : c + lanes], h[r + b : r + 2 * b, c : c + lanes]
        )
        scr[pl.ds(j * (b + 1), b), :] = quad(0, 0) + (quad(0, lanes) + quad(2 * b, 0))
        return carry

    lax.fori_loop(0, tile, collect, 0, unroll=tile)
    keep_t = lane_half(tile, lanes)
    for r in range(0, block_size, 2):
        even = scr[pl.ds(r, tile, stride=block_size + 1), :]
        odd = scr[pl.ds(r + 1, tile, stride=block_size + 1), :]
        columns = slice(r * block_size, (r + 2) * block_size)
        out_ref[0, :, columns] = jnp.where(keep_t, even, pltpu.roll(odd, block_size, 1)).astype(BF16)
        out_ref[1, :, columns] = jnp.where(keep_t, pltpu.roll(even, block_size, 1), odd).astype(BF16)

def whole(shape):
    return pl.BlockSpec(shape, lambda *_: (0,) * len(shape))


def cost(us, count):
    return pl.CostEstimate(flops=us * 10**9, bytes_accessed=count, transcendentals=0)


def group_table(x, y, panel, positions, own, block_count):
    count, width = panel.shape
    b = x.shape[0] // block_count
    tile = math.gcd(count, 32)
    return pl.pallas_call(
        functools.partial(group_kernel, block_count, tile),
        grid_spec=pltpu.PrefetchScalarGridSpec(
            num_scalar_prefetch=2,
            grid=(count // tile,),
            in_specs=[
                whole(x.shape),
                whole(y.shape),
                pl.BlockSpec((tile, width), lambda i, *_: (i, 0)),
            ],
            out_specs=pl.BlockSpec((2, tile, width), lambda i, *_: (0, i, 0)),
            scratch_shapes=[
                pltpu.VMEM((block_count, 4 * b, 2 * b), BF16),
                pltpu.VMEM((block_count, 2 * b, 4 * b), BF16),
                pltpu.VMEM((tile * (b + 1) + 7, 2 * b), F32),
                pltpu.VMEM((tile * (b + 1) + 7, 2 * b), F32),
                pltpu.VMEM((tile, 4 * b, 4 * b), BF16),
            ],
        ),
        out_shape=jax.ShapeDtypeStruct((2, count, width), BF16),
        cost_estimate=cost(25, 10**7),
        name="group_table",
    )(positions, own, x, y, panel)


def own_kernel(block_count, pos_ref, x_ref, y_ref, panel_ref, out_ref, left, right, pairs, mid, scr):
    step = pl.program_id(0)
    count = panel_ref.shape[0]
    order = x_ref.shape[0]
    b = order // block_count
    lanes = 2 * b
    pitch = b + 1

    @pl.when(step == 0)
    def _():
        for p in range(block_count):
            cols = slice(p * b, (p + 1) * b)
            high, low = split(jnp.concatenate([x_ref[:, cols], y_ref[:, cols]], axis=1))
            left[p, :, :lanes] = high
            left[p, :, lanes:] = low
        for m, ref in enumerate((y_ref, x_ref)):
            for q in range(block_count):
                high, low = split(ref[q * b : (q + 1) * b, :])
                cols = slice(m * order, (m + 1) * order)
                right[q, :b, cols] = high
                right[q, b:, cols] = low
        unpack_pairs(panel_ref, pairs, count, b)

    dot = functools.partial(jnp.dot, preferred_element_type=F32)
    position = pos_ref[step]
    p = position // block_count
    q = position % block_count
    block = pairs[pl.ds(step * pitch, b), :]
    turned = jnp.concatenate([block, block], axis=0).T[:b]
    top = dot(block.astype(BF16), right[q])
    low_part = dot(turned.astype(BF16), right[p])
    for m, part in enumerate((top[:, :order], top[:, order:], low_part[:, :order], low_part[:, order:])):
        high, low = split(part)
        mid[m * b : (m + 1) * b, :] = high
        mid[(8 + m) * b : (9 + m) * b, :] = low
    mid[4 * b : 8 * b, :] = mid[: 4 * b, :]
    lp, lq = left[p], left[q]
    a = jnp.concatenate([lp[:, :lanes], lq[:, :lanes]], axis=1)
    a_low = jnp.concatenate([lp[:, lanes:], lq[:, lanes:]], axis=1)
    a = jnp.concatenate([a, a_low, a], axis=1)
    groups = order // lanes
    for g in range(groups):
        h = dot(a, mid[:, g * lanes : (g + 1) * lanes])
        for i in range(block_count):
            start = (g * block_count + i) * pitch
            scr[start : start + b, :] = h[i * b : (i + 1) * b]
    keep = lane_half(block_count, lanes)
    for g in range(groups):
        base = g * block_count * pitch
        for r in range(0, b, 2):
            even = scr[pl.ds(base + r, block_count, stride=pitch), :]
            odd = scr[pl.ds(base + r + 1, block_count, stride=pitch), :]
            one = jnp.where(keep, even, pltpu.roll(odd, b, 1))
            two = jnp.where(keep, pltpu.roll(even, b, 1), odd)
            out_ref[
                2 * g * block_count : 2 * (g + 1) * block_count, r * b : (r + 2) * b
            ] = jnp.concatenate([one, two], axis=0).astype(BF16)


def own_table(x, y, panel, positions, block_count):
    count, width = panel.shape
    order = x.shape[0]
    b = order // block_count
    rows = block_count * block_count
    return pl.pallas_call(
        functools.partial(own_kernel, block_count),
        grid_spec=pltpu.PrefetchScalarGridSpec(
            num_scalar_prefetch=1,
            grid=(count,),
            in_specs=[whole(x.shape), whole(y.shape), whole(panel.shape)],
            out_specs=pl.BlockSpec((rows, width), lambda i, *_: (i, 0)),
            scratch_shapes=[
                pltpu.VMEM((block_count, order, 4 * b), BF16),
                pltpu.VMEM((block_count, 2 * b, 2 * order), BF16),
                pltpu.VMEM((max(count, 8) * (b + 1) + 7, 2 * b), F32),
                pltpu.VMEM((12 * b, order), BF16),
                pltpu.VMEM((order // 2 // b * block_count * (b + 1) + 7, 2 * b), F32),
            ],
        ),
        out_shape=jax.ShapeDtypeStruct((count * rows, width), BF16),
        cost_estimate=cost(15, 10**7),
        name="own_table",
    )(positions, x, y, panel)


def row_kernel(cons_ref, table_ref, block_ref, place_ref, out_ref, total):
    step = pl.program_id(0)
    nt = (((1,), (1,)), ((), ()))
    cons = cons_ref[...]
    rows = lax.dot_general(cons, table_ref[0], nt, preferred_element_type=F32)
    block = block_ref[...]
    for s in range(1, table_ref.shape[0]):
        other = lax.dot_general(cons, table_ref[s], nt, preferred_element_type=F32)
        rows = jnp.where(block == s, other, rows)
    rows = rows.astype(BF16)
    places, tile = total.shape[0], cons.shape[0]
    hits = lax.broadcasted_iota(jnp.int32, (places, tile), 0) == place_ref[...]
    part = jnp.dot(jnp.where(hits, 1.0, 0.0).astype(BF16), rows, preferred_element_type=F32)

    @pl.when(step == 0)
    def _():
        total[...] = part

    @pl.when(step > 0)
    def _():
        total[...] += part

    @pl.when(step == pl.num_programs(0) - 1)
    def _():
        out_ref[...] = total[...].astype(BF16)


def send_rows(cons, table, block, place, places):
    slots, width = cons.shape
    cols = table.shape[1]
    tile = math.gcd(slots, 256)
    return pl.pallas_call(
        row_kernel,
        grid=(slots // tile,),
        in_specs=[
            pl.BlockSpec((tile, width), lambda i: (i, 0)),
            pl.BlockSpec(table.shape, lambda i: (0, 0, 0), pipeline_mode=pl.Buffered(1)),
            pl.BlockSpec((tile, 1), lambda i: (i, 0)),
            pl.BlockSpec((1, tile), lambda i: (0, i)),
        ],
        out_specs=whole((places, cols)),
        out_shape=jax.ShapeDtypeStruct((places, cols), BF16),
        scratch_shapes=[pltpu.VMEM((places, cols), F32)],
        cost_estimate=cost(20, 2 * 10**7),
        name="send_rows",
    )(cons, table, block.reshape(-1, 1), place.reshape(1, -1))


def update_kernel(parts, *refs):
    row_refs, (weight_ref, trailing_ref, out_ref) = refs[:parts], refs[parts:]
    rows = jnp.concatenate([ref[...] for ref in row_refs] * 2, axis=1)
    out_ref[...] = trailing_ref[...] - jnp.dot(rows, weight_ref[...], preferred_element_type=F32)


def update(row_parts, weight, trailing):
    rows, cols = trailing.shape
    tile = math.gcd(rows, 512)
    return pl.pallas_call(
        functools.partial(update_kernel, len(row_parts)),
        grid=(rows // tile,),
        in_specs=[pl.BlockSpec((tile, part.shape[1]), lambda i: (i, 0)) for part in row_parts]
        + [whole(weight.shape), pl.BlockSpec((tile, cols), lambda i: (i, 0))],
        out_specs=pl.BlockSpec((tile, cols), lambda i: (i, 0)),
        out_shape=jax.ShapeDtypeStruct((rows, cols), F32),
        cost_estimate=cost(8, 2 * 10**7),
        name="update",
    )(*row_parts, weight, trailing)


def hdot(a, b, contract):
    return lax.dot_general(
        a, b, ((contract[:1], contract[1:]), ((), ())),
        precision=lax.Precision.HIGHEST, preferred_element_type=F32,
    )


def factor_kernel(block, s_ref, out_ref, a, work):
    order = s_ref.shape[0]
    count = order // block
    groups = block // 8
    a[...] = s_ref[...]
    row_id = lax.broadcasted_iota(jnp.int32, (8, 1), 0)
    eye = (
        lax.broadcasted_iota(jnp.int32, (block, block), 0)
        == lax.broadcasted_iota(jnp.int32, (block, block), 1)
    ).astype(F32)

    def diagonal(b, carry):
        start = pl.multiple_of(b * block, block)
        work[:, :block] = a[pl.ds(start, block), pl.ds(start, block)]
        work[:, block:] = eye
        rows = [work[8 * g : 8 * g + 8, :] for g in range(groups)]
        for k in range(block):
            g, s = divmod(k, 8)
            pivot_row = rows[g][s : s + 1, :]
            d = pivot_row[:, k : k + 1]
            inv = lax.rsqrt(d)
            inv = inv * (1.5 - 0.5 * d * inv * inv)
            scaled = pivot_row * inv
            for i in range(g, groups):
                mult = rows[i][:, k : k + 1] * inv
                if i == g:
                    mult = jnp.where(row_id > s, mult, 0.0)
                    rows[i] = jnp.where(row_id == s, scaled, rows[i] - mult * scaled)
                else:
                    rows[i] = rows[i] - mult * scaled
        inverse = jnp.concatenate([row[:, block:] for row in rows], axis=0)
        out_ref[pl.ds(start, block), pl.ds(start, block)] = inverse
        panel = hdot(a[:, pl.ds(start, block)], inverse, (1, 1))
        below = lax.broadcasted_iota(jnp.int32, (order, 1), 0) >= start + block
        panel = jnp.where(below, panel, 0.0)
        a[:, pl.ds(start, block)] = panel
        return carry, panel

    def body(b, carry):
        _, panel = diagonal(b, carry)
        start = pl.multiple_of(b * block, block)

        for i in range(1, count):
            @pl.when(b < i)
            def _():
                piece = a[i * block : (i + 1) * block, pl.ds(start, block)]
                cols = slice(i * block, (i + 1) * block)
                a[:, cols] = a[:, cols] - hdot(panel, piece, (1, 1))

        return carry

    lax.fori_loop(0, count, body, 0)
    for i in range(count):
        for b in range(i + 1, count):
            out_ref[i * block : (i + 1) * block, b * block : (b + 1) * block] = jnp.zeros(
                (block, block), F32
            )
    for i in range(1, count):
        low_row = a[i * block : (i + 1) * block, : i * block]
        total = hdot(low_row, out_ref[: i * block, : i * block], (1, 0))
        own = out_ref[i * block : (i + 1) * block, i * block : (i + 1) * block]
        out_ref[i * block : (i + 1) * block, : i * block] = -hdot(own, total, (1, 0))


def inverse_factor(matrix):
    order = matrix.shape[0]
    block = 128
    return pl.pallas_call(
        functools.partial(factor_kernel, block),
        in_specs=[pl.BlockSpec(memory_space=pltpu.VMEM)],
        out_specs=pl.BlockSpec(memory_space=pltpu.VMEM),
        out_shape=jax.ShapeDtypeStruct((order, order), F32),
        scratch_shapes=[pltpu.VMEM((order, order), F32), pltpu.VMEM((block, 2 * block), F32)],
        cost_estimate=pl.CostEstimate(
            flops=60 * 10**9, bytes_accessed=2 * 10**6, transcendentals=order
        ),
        name="inverse_factor",
    )(matrix)


def body(
    x_mat,
    y_inv,
    panel_blocks,
    panel_pos,
    group_blocks,
    cons_blocks,
    slot_block,
    slot_row,
    group_size,
    trailing,
):
    rows_size = lax.axis_size("row")
    cols_size = lax.axis_size("col")
    devices = rows_size * cols_size
    col_index = lax.axis_index("col")
    device_id = lax.axis_index("row") * cols_size + col_index
    panel_cols = panel_blocks.shape[0]
    per_device = panel_cols // devices
    order = x_mat.shape[0]
    block_size = math.isqrt(panel_blocks.shape[1])
    block_count = order // block_size
    slot_count = cons_blocks.shape[0]

    sub_rows = trailing.shape[0] // cols_size
    base_share = sub_rows // devices
    spread = sub_rows - devices // 4 * base_share
    capacity = base_share + (spread + devices - 1) // devices
    places = devices * capacity
    slot_ids = jnp.arange(slot_count, dtype=jnp.int32)
    live_slots = slot_ids < group_size[0]
    target = slot_row // sub_rows
    dest_hits = (
        target[:, None] == jnp.arange(devices, dtype=jnp.int32)[None, :]
    ) & live_slots[:, None]
    earlier = (slot_ids[:, None] > slot_ids[None, :]).astype(BF16)
    before = jnp.dot(earlier, dest_hits.astype(BF16), preferred_element_type=F32)
    dest_rank = jnp.sum(jnp.where(dest_hits, before, 0.0), axis=1).astype(jnp.int32)
    slot_place = jnp.where(live_slots, target * capacity + dest_rank, places)
    place_ids = jnp.arange(places, dtype=jnp.int32)
    tag = slot_row % sub_rows + 1
    digits = jnp.stack([tag // 32, tag % 32], axis=1).astype(BF16)
    sent_digits = jnp.dot(
        (place_ids[:, None] == slot_place[None, :]).astype(BF16), digits, preferred_element_type=F32
    ).astype(jnp.int32)
    send_local = sent_digits[:, 0] * 32 + sent_digits[:, 1] - 1
    exchange = functools.partial(
        lax.all_to_all, axis_name=("row", "col"), split_axis=0, concat_axis=0, tiled=True
    )
    recv_local = exchange(send_local.reshape(devices, capacity))

    own_panel = lax.dynamic_slice_in_dim(panel_blocks, device_id * per_device, per_device, 0)
    own_pos = lax.dynamic_slice_in_dim(panel_pos, device_id * per_device, per_device, 0)
    own_rows = own_table(x_mat, y_inv, own_panel, own_pos, block_count)
    products = lax.dot_general(
        own_rows, panel_blocks, (((1,), (1,)), ((), ())), preferred_element_type=F32
    )
    place = panel_pos % block_count * block_count + panel_pos // block_count
    position_count = block_count * block_count
    hit = jnp.arange(position_count, dtype=jnp.int32)[:, None] == place[None, :]
    row_part = jnp.sum(
        jnp.where(hit[None], products.reshape(per_device, position_count, panel_cols), 0.0), axis=1
    )
    column_part = lax.all_gather(row_part, "col", axis=0, tiled=True)
    panel_schur = lax.all_gather(column_part, "row", axis=0, tiled=True)

    own_group = lax.dynamic_index_in_dim(group_blocks, device_id, 0, keepdims=False)
    halves = 2
    width = panel_cols // halves
    token = row_part
    local_ids = jnp.arange(sub_rows, dtype=jnp.int32)
    slabs, gathered = [], []
    for half in range(halves):
        cols = slice(half * width, (half + 1) * width)
        x_now, token = lax.optimization_barrier((x_mat, token))
        table = group_table(x_now, y_inv, panel_blocks[cols], panel_pos[cols], own_group, block_count)
        sent = send_rows(cons_blocks, table, slot_block, slot_place, places)
        token = sent
        received = exchange(sent.reshape(devices, capacity, width))
        recv_hits = (local_ids[:, None] == recv_local.reshape(1, -1)).astype(BF16)
        slab = jnp.dot(
            recv_hits, received.reshape(-1, width), preferred_element_type=F32
        ).astype(BF16)
        slabs.append(slab)
        gathered.append(lax.all_gather(slab, "col", axis=0, tiled=True))

    block_rows = trailing.shape[1] // rows_size
    slab = jnp.concatenate(slabs, axis=1)
    head = slab[: block_rows * cols_size].reshape(cols_size, block_rows, panel_cols)
    head = lax.all_to_all(head, "col", split_axis=0, concat_axis=0, tiled=True)[0]
    picked = lax.all_to_all(
        jnp.broadcast_to(head[None], (rows_size, block_rows, panel_cols)),
        "row", split_axis=0, concat_axis=0, tiled=True,
    ).reshape(rows_size * block_rows, panel_cols)

    panel_schur, token = lax.optimization_barrier((panel_schur, token))
    symmetric = 0.5 * (panel_schur + panel_schur.T)
    eye = (
        lax.broadcasted_iota(jnp.int32, symmetric.shape, 0)
        == lax.broadcasted_iota(jnp.int32, symmetric.shape, 1)
    )
    diag_shift = 0.01 * jnp.sum(jnp.where(eye, symmetric, 0.0)) / panel_cols
    inverse = inverse_factor(symmetric + jnp.where(eye, diag_shift, 0.0))
    inner = hdot(inverse, inverse, (0, 0))

    def doubled(matrix):
        rounded = lax.reduce_precision(matrix, exponent_bits=8, mantissa_bits=7)
        low = lax.reduce_precision(matrix - rounded, exponent_bits=8, mantissa_bits=7)
        return jnp.concatenate([rounded.astype(BF16), low.astype(BF16)], axis=1)

    lower_slab = lax.dot_general(
        jnp.concatenate([slab, slab], axis=1), doubled(inverse), (((1,), (1,)), ((), ())),
        preferred_element_type=F32,
    )
    weight = lax.dot_general(
        doubled(inner), jnp.concatenate([picked, picked], axis=1), (((1,), (1,)), ((), ())),
        preferred_element_type=F32,
    )
    weight = doubled(weight.T).T
    return (lower_slab, update(gathered, weight, trailing))


def solution(mesh):
    return jax.shard_map(
        body,
        mesh=mesh,
        in_specs=(
            P(),
            P(),
            P(),
            P(),
            P(),
            P(("row", "col"), None),
            P(("row", "col")),
            P(("row", "col")),
            P(("row", "col")),
            P("row", "col"),
        ),
        out_specs=(P(("row", "col"), None), P("row", "col")),
        check_vma=False,
    )
```

```python
import functools
import math

import jax
import jax.numpy as jnp
from jax import lax
from jax.experimental import pallas as pl
from jax.experimental.pallas import tpu as pltpu
from jax.sharding import PartitionSpec as P


BF16 = jnp.bfloat16
F32 = jnp.float32


def split(value):
    high = value.astype(BF16)
    low = (value - high.astype(F32)).astype(BF16)
    return high, low


def lane_half(rows, width):
    return lax.broadcasted_iota(jnp.int32, (rows, width), 1) < width // 2


def unpack_pairs(panel_ref, pairs, count, block_size):
    lanes = 2 * block_size
    keep = lane_half(count, lanes)
    for c in range(block_size // 2):
        both = panel_ref[:, c * lanes : (c + 1) * lanes].astype(F32)
        turned = pltpu.roll(both, block_size, 1)
        pitch = block_size + 1
        pairs[pl.ds(2 * c, count, stride=pitch), :] = jnp.where(keep, both, turned)
        pairs[pl.ds(2 * c + 1, count, stride=pitch), :] = jnp.where(keep, turned, both)


def column_block(ref, block, slot, block_size):
    lanes = 2 * block_size
    start = pl.multiple_of(block // 2 * lanes, lanes)
    wide = ref[:, pl.ds(start, lanes)]
    return jnp.where(block % 2 == slot, wide, pltpu.roll(wide, block_size, 1))


def group_kernel(block_count, tile, pos_ref, own_ref, x_ref, y_ref, panel_ref, out_ref, left, right, pairs, scr, mid):
    step = pl.program_id(0)
    order = x_ref.shape[0]
    block_size = order // block_count
    lanes = 2 * block_size
    half = lane_half(order, lanes)

    @pl.when(step == 0)
    def _():
        for s in range(2):
            position = own_ref[s]
            a = pl.multiple_of(position // block_count * block_size, block_size)
            xa = x_ref[pl.ds(a, block_size), :]
            ya = y_ref[pl.ds(a, block_size), :]
            for p in range(block_count):
                cols = slice(p * block_size, (p + 1) * block_size)
                high, low = split(jnp.concatenate([xa[:, cols], ya[:, cols]], axis=1))
                left[p, s * block_size : (s + 1) * block_size, :] = high
                left[p, (2 + s) * block_size : (3 + s) * block_size, :] = low
        for m, ref in enumerate((y_ref, x_ref)):
            first = column_block(ref, own_ref[0] % block_count, 0, block_size)
            second = column_block(ref, own_ref[1] % block_count, 1, block_size)
            high, low = split(jnp.where(half, first, second))
            for q in range(block_count):
                rows = slice(q * block_size, (q + 1) * block_size)
                cols = slice(m * lanes, (m + 1) * lanes)
                right[q, :block_size, cols] = high[rows]
                right[q, block_size:, cols] = low[rows]

    unpack_pairs(panel_ref, pairs, tile, block_size)
    keep = lane_half(block_size, lanes)
    dot = functools.partial(jnp.dot, preferred_element_type=F32)

    def spread(j, e, t):
        position = pos_ref[step * tile + j]
        p = position // block_count
        q = position % block_count
        top = dot(e, right[q])
        low_part = dot(t, right[p])
        for m, part in enumerate((top[:, :lanes], top[:, lanes:], low_part[:, :lanes], low_part[:, lanes:])):
            high, low = split(part)
            rows = slice(m * block_size, (m + 1) * block_size)
            mid[j, rows, :lanes] = high
            mid[j, rows, lanes:] = low

    def two(i, carry):
        pitch = block_size + 1
        block = jnp.concatenate(
            [pairs[pl.ds(2 * i * pitch, block_size), :], pairs[pl.ds((2 * i + 1) * pitch, block_size), :]],
            axis=0,
        )
        turned = block.T[:block_size]
        swapped = pltpu.roll(turned, block_size, 1)
        e = block.astype(BF16)
        spread(2 * i, e[:block_size], jnp.where(keep, turned, swapped).astype(BF16))
        spread(2 * i + 1, e[block_size:], jnp.where(keep, swapped, turned).astype(BF16))
        return carry

    lax.fori_loop(0, tile // 2, two, 0, unroll=tile // 2)

    def collect(j, carry):
        position = pos_ref[step * tile + j]
        a = jnp.concatenate([left[position // block_count], left[position % block_count]], axis=1)
        h = dot(a, mid[j])
        b = block_size
        quad = lambda r, c: jnp.where(
            keep, h[r : r + b, c : c + lanes], h[r + b : r + 2 * b, c : c + lanes]
        )
        scr[pl.ds(j * (b + 1), b), :] = quad(0, 0) + (quad(0, lanes) + quad(2 * b, 0))
        return carry

    lax.fori_loop(0, tile, collect, 0, unroll=tile)
    keep_t = lane_half(tile, lanes)
    for r in range(0, block_size, 2):
        even = scr[pl.ds(r, tile, stride=block_size + 1), :]
        odd = scr[pl.ds(r + 1, tile, stride=block_size + 1), :]
        columns = slice(r * block_size, (r + 2) * block_size)
        out_ref[0, :, columns] = jnp.where(keep_t, even, pltpu.roll(odd, block_size, 1)).astype(BF16)
        out_ref[1, :, columns] = jnp.where(keep_t, pltpu.roll(even, block_size, 1), odd).astype(BF16)


def whole(shape):
    return pl.BlockSpec(shape, lambda *_: (0,) * len(shape))


def cost(us, count):
    return pl.CostEstimate(flops=us * 10**9, bytes_accessed=count, transcendentals=0)


def group_table(x, y, panel, positions, own, block_count):
    count, width = panel.shape
    b = x.shape[0] // block_count
    tile = math.gcd(count, 32)
    return pl.pallas_call(
        functools.partial(group_kernel, block_count, tile),
        grid_spec=pltpu.PrefetchScalarGridSpec(
            num_scalar_prefetch=2,
            grid=(count // tile,),
            in_specs=[
                whole(x.shape),
                whole(y.shape),
                pl.BlockSpec((tile, width), lambda i, *_: (i, 0)),
            ],
            out_specs=pl.BlockSpec((2, tile, width), lambda i, *_: (0, i, 0)),
            scratch_shapes=[
                pltpu.VMEM((block_count, 4 * b, 2 * b), BF16),
                pltpu.VMEM((block_count, 2 * b, 4 * b), BF16),
                pltpu.VMEM((tile * (b + 1) + 7, 2 * b), F32),
                pltpu.VMEM((tile * (b + 1) + 7, 2 * b), F32),
                pltpu.VMEM((tile, 4 * b, 4 * b), BF16),
            ],
        ),
        out_shape=jax.ShapeDtypeStruct((2, count, width), BF16),
        cost_estimate=cost(25, 10**7),
        name="group_table",
    )(positions, own, x, y, panel)


def own_kernel(block_count, pos_ref, x_ref, y_ref, panel_ref, out_ref, left, right, pairs, mid, scr):
    step = pl.program_id(0)
    count = panel_ref.shape[0]
    order = x_ref.shape[0]
    b = order // block_count
    lanes = 2 * b
    pitch = b + 1

    @pl.when(step == 0)
    def _():
        for p in range(block_count):
            cols = slice(p * b, (p + 1) * b)
            high, low = split(jnp.concatenate([x_ref[:, cols], y_ref[:, cols]], axis=1))
            left[p, :, :lanes] = high
            left[p, :, lanes:] = low
        for m, ref in enumerate((y_ref, x_ref)):
            for q in range(block_count):
                high, low = split(ref[q * b : (q + 1) * b, :])
                cols = slice(m * order, (m + 1) * order)
                right[q, :b, cols] = high
                right[q, b:, cols] = low
        unpack_pairs(panel_ref, pairs, count, b)

    dot = functools.partial(jnp.dot, preferred_element_type=F32)
    position = pos_ref[step]
    p = position // block_count
    q = position % block_count
    block = pairs[pl.ds(step * pitch, b), :]
    turned = jnp.concatenate([block, block], axis=0).T[:b]
    top = dot(block.astype(BF16), right[q])
    low_part = dot(turned.astype(BF16), right[p])
    for m, part in enumerate((top[:, :order], top[:, order:], low_part[:, :order], low_part[:, order:])):
        high, low = split(part)
        mid[m * b : (m + 1) * b, :] = high
        mid[(8 + m) * b : (9 + m) * b, :] = low
    mid[4 * b : 8 * b, :] = mid[: 4 * b, :]
    lp, lq = left[p], left[q]
    a = jnp.concatenate([lp[:, :lanes], lq[:, :lanes]], axis=1)
    a_low = jnp.concatenate([lp[:, lanes:], lq[:, lanes:]], axis=1)
    a = jnp.concatenate([a, a_low, a], axis=1)
    groups = order // lanes
    for g in range(groups):
        h = dot(a, mid[:, g * lanes : (g + 1) * lanes])
        for i in range(block_count):
            start = (g * block_count + i) * pitch
            scr[start : start + b, :] = h[i * b : (i + 1) * b]
    keep = lane_half(block_count, lanes)
    for g in range(groups):
        base = g * block_count * pitch
        for r in range(0, b, 2):
            even = scr[pl.ds(base + r, block_count, stride=pitch), :]
            odd = scr[pl.ds(base + r + 1, block_count, stride=pitch), :]
            one = jnp.where(keep, even, pltpu.roll(odd, b, 1))
            two = jnp.where(keep, pltpu.roll(even, b, 1), odd)
            out_ref[
                2 * g * block_count : 2 * (g + 1) * block_count, r * b : (r + 2) * b
            ] = jnp.concatenate([one, two], axis=0).astype(BF16)


def own_table(x, y, panel, positions, block_count):
    count, width = panel.shape
    order = x.shape[0]
    b = order // block_count
    rows = block_count * block_count
    return pl.pallas_call(
        functools.partial(own_kernel, block_count),
        grid_spec=pltpu.PrefetchScalarGridSpec(
            num_scalar_prefetch=1,
            grid=(count,),
            in_specs=[whole(x.shape), whole(y.shape), whole(panel.shape)],
            out_specs=pl.BlockSpec((rows, width), lambda i, *_: (i, 0)),
            scratch_shapes=[
                pltpu.VMEM((block_count, order, 4 * b), BF16),
                pltpu.VMEM((block_count, 2 * b, 2 * order), BF16),
                pltpu.VMEM((max(count, 8) * (b + 1) + 7, 2 * b), F32),
                pltpu.VMEM((12 * b, order), BF16),
                pltpu.VMEM((order // 2 // b * block_count * (b + 1) + 7, 2 * b), F32),
            ],
        ),
        out_shape=jax.ShapeDtypeStruct((count * rows, width), BF16),
        cost_estimate=cost(15, 10**7),
        name="own_table",
    )(positions, x, y, panel)


def row_kernel(cons_ref, table_ref, block_ref, place_ref, out_ref, total):
    step = pl.program_id(0)
    nt = (((1,), (1,)), ((), ()))
    cons = cons_ref[...]
    rows = lax.dot_general(cons, table_ref[0], nt, preferred_element_type=F32)
    block = block_ref[...]
    for s in range(1, table_ref.shape[0]):
        other = lax.dot_general(cons, table_ref[s], nt, preferred_element_type=F32)
        rows = jnp.where(block == s, other, rows)
    rows = rows.astype(BF16)
    places, tile = total.shape[0], cons.shape[0]
    hits = lax.broadcasted_iota(jnp.int32, (places, tile), 0) == place_ref[...]
    part = jnp.dot(jnp.where(hits, 1.0, 0.0).astype(BF16), rows, preferred_element_type=F32)

    @pl.when(step == 0)
    def _():
        total[...] = part

    @pl.when(step > 0)
    def _():
        total[...] += part

    @pl.when(step == pl.num_programs(0) - 1)
    def _():
        out_ref[...] = total[...].astype(BF16)


def send_rows(cons, table, block, place, places):
    slots, width = cons.shape
    cols = table.shape[1]
    tile = math.gcd(slots, 256)
    return pl.pallas_call(
        row_kernel,
        grid=(slots // tile,),
        in_specs=[
            pl.BlockSpec((tile, width), lambda i: (i, 0)),
            pl.BlockSpec(table.shape, lambda i: (0, 0, 0), pipeline_mode=pl.Buffered(1)),
            pl.BlockSpec((tile, 1), lambda i: (i, 0)),
            pl.BlockSpec((1, tile), lambda i: (0, i)),
        ],
        out_specs=whole((places, cols)),
        out_shape=jax.ShapeDtypeStruct((places, cols), BF16),
        scratch_shapes=[pltpu.VMEM((places, cols), F32)],
        cost_estimate=cost(20, 2 * 10**7),
        name="send_rows",
    )(cons, table, block.reshape(-1, 1), place.reshape(1, -1))


def update_kernel(parts, *refs):
    row_refs, (weight_ref, trailing_ref, out_ref) = refs[:parts], refs[parts:]
    rows = jnp.concatenate([ref[...] for ref in row_refs] * 2, axis=1)
    out_ref[...] = trailing_ref[...] - jnp.dot(rows, weight_ref[...], preferred_element_type=F32)


def update(row_parts, weight, trailing):
    rows, cols = trailing.shape
    tile = math.gcd(rows, 512)
    return pl.pallas_call(
        functools.partial(update_kernel, len(row_parts)),
        grid=(rows // tile,),
        in_specs=[pl.BlockSpec((tile, part.shape[1]), lambda i: (i, 0)) for part in row_parts]
        + [whole(weight.shape), pl.BlockSpec((tile, cols), lambda i: (i, 0))],
        out_specs=pl.BlockSpec((tile, cols), lambda i: (i, 0)),
        out_shape=jax.ShapeDtypeStruct((rows, cols), F32),
        cost_estimate=cost(8, 2 * 10**7),
        name="update",
    )(*row_parts, weight, trailing)


def hdot(a, b, contract):
    return lax.dot_general(
        a, b, ((contract[:1], contract[1:]), ((), ())),
        precision=lax.Precision.HIGHEST, preferred_element_type=F32,
    )


def factor_kernel(block, begin, end, finish, *refs):
    if finish:
        s_ref, done_ref, out_ref, a, work = refs
    else:
        s_ref, a, out_ref, work = refs
    order = s_ref.shape[0]
    count = order // block
    groups = block // 8
    a[...] = s_ref[...]
    if finish:
        out_ref[...] = done_ref[...]
    row_id = lax.broadcasted_iota(jnp.int32, (8, 1), 0)
    eye = (
        lax.broadcasted_iota(jnp.int32, (block, block), 0)
        == lax.broadcasted_iota(jnp.int32, (block, block), 1)
    ).astype(F32)

    def diagonal(b, carry):
        start = pl.multiple_of(b * block, block)
        work[:, :block] = a[pl.ds(start, block), pl.ds(start, block)]
        work[:, block:] = eye
        rows = [work[8 * g : 8 * g + 8, :] for g in range(groups)]
        for k in range(block):
            g, s = divmod(k, 8)
            pivot_row = rows[g][s : s + 1, :]
            d = pivot_row[:, k : k + 1]
            inv = lax.rsqrt(d)
            inv = inv * (1.5 - 0.5 * d * inv * inv)
            scaled = pivot_row * inv
            for i in range(g, groups):
                mult = rows[i][:, k : k + 1] * inv
                if i == g:
                    mult = jnp.where(row_id > s, mult, 0.0)
                    rows[i] = jnp.where(row_id == s, scaled, rows[i] - mult * scaled)
                else:
                    rows[i] = rows[i] - mult * scaled
        inverse = jnp.concatenate([row[:, block:] for row in rows], axis=0)
        out_ref[pl.ds(start, block), pl.ds(start, block)] = inverse
        panel = hdot(a[:, pl.ds(start, block)], inverse, (1, 1))
        below = lax.broadcasted_iota(jnp.int32, (order, 1), 0) >= start + block
        panel = jnp.where(below, panel, 0.0)
        a[:, pl.ds(start, block)] = panel
        return carry, panel

    def body(b, carry):
        _, panel = diagonal(b, carry)
        start = pl.multiple_of(b * block, block)

        for i in range(1, count):
            @pl.when(b < i)
            def _():
                piece = a[i * block : (i + 1) * block, pl.ds(start, block)]
                cols = slice(i * block, (i + 1) * block)
                a[:, cols] = a[:, cols] - hdot(panel, piece, (1, 1))

        return carry

    lax.fori_loop(begin, end, body, 0)
    if not finish:
        return
    for i in range(count):
        for b in range(i + 1, count):
            out_ref[i * block : (i + 1) * block, b * block : (b + 1) * block] = jnp.zeros(
                (block, block), F32
            )
    for i in range(1, count):
        low_row = a[i * block : (i + 1) * block, : i * block]
        total = hdot(low_row, out_ref[: i * block, : i * block], (1, 0))
        own = out_ref[i * block : (i + 1) * block, i * block : (i + 1) * block]
        out_ref[i * block : (i + 1) * block, : i * block] = -hdot(own, total, (1, 0))


def factor_start(matrix):
    order = matrix.shape[0]
    block = 128
    shape = jax.ShapeDtypeStruct((order, order), F32)
    return pl.pallas_call(
        functools.partial(factor_kernel, block, 0, order // block // 2, False),
        in_specs=[pl.BlockSpec(memory_space=pltpu.VMEM)],
        out_specs=[pl.BlockSpec(memory_space=pltpu.VMEM)] * 2,
        out_shape=[shape, shape],
        scratch_shapes=[pltpu.VMEM((block, 2 * block), F32)],
        cost_estimate=cost(30, 10**6),
        name="factor_start",
    )(matrix)


def factor_end(matrix, done):
    order = matrix.shape[0]
    block = 128
    return pl.pallas_call(
        functools.partial(factor_kernel, block, order // block // 2, order // block, True),
        in_specs=[pl.BlockSpec(memory_space=pltpu.VMEM)] * 2,
        out_specs=pl.BlockSpec(memory_space=pltpu.VMEM),
        out_shape=jax.ShapeDtypeStruct((order, order), F32),
        scratch_shapes=[pltpu.VMEM((order, order), F32), pltpu.VMEM((block, 2 * block), F32)],
        cost_estimate=cost(30, 10**6),
        name="factor_end",
    )(matrix, done)


def body(
    x_mat,
    y_inv,
    panel_blocks,
    panel_pos,
    group_blocks,
    cons_blocks,
    slot_block,
    slot_row,
    group_size,
    trailing,
):
    rows_size = lax.axis_size("row")
    cols_size = lax.axis_size("col")
    devices = rows_size * cols_size
    col_index = lax.axis_index("col")
    device_id = lax.axis_index("row") * cols_size + col_index
    panel_cols = panel_blocks.shape[0]
    per_device = panel_cols // devices
    order = x_mat.shape[0]
    block_size = math.isqrt(panel_blocks.shape[1])
    block_count = order // block_size
    slot_count = cons_blocks.shape[0]

    sub_rows = trailing.shape[0] // cols_size
    base_share = sub_rows // devices
    spread = sub_rows - devices // 4 * base_share
    capacity = base_share + (spread + devices - 1) // devices
    places = devices * capacity
    slot_ids = jnp.arange(slot_count, dtype=jnp.int32)
    live_slots = slot_ids < group_size[0]
    target = slot_row // sub_rows
    dest_hits = (
        target[:, None] == jnp.arange(devices, dtype=jnp.int32)[None, :]
    ) & live_slots[:, None]
    earlier = (slot_ids[:, None] > slot_ids[None, :]).astype(BF16)
    before = jnp.dot(earlier, dest_hits.astype(BF16), preferred_element_type=F32)
    dest_rank = jnp.sum(jnp.where(dest_hits, before, 0.0), axis=1).astype(jnp.int32)
    slot_place = jnp.where(live_slots, target * capacity + dest_rank, places)
    place_ids = jnp.arange(places, dtype=jnp.int32)
    tag = slot_row % sub_rows + 1
    digits = jnp.stack([tag // 32, tag % 32], axis=1).astype(BF16)
    sent_digits = jnp.dot(
        (place_ids[:, None] == slot_place[None, :]).astype(BF16), digits, preferred_element_type=F32
    ).astype(jnp.int32)
    send_local = sent_digits[:, 0] * 32 + sent_digits[:, 1] - 1
    exchange = functools.partial(
        lax.all_to_all, axis_name=("row", "col"), split_axis=0, concat_axis=0, tiled=True
    )
    recv_local = exchange(send_local.reshape(devices, capacity))

    own_panel = lax.dynamic_slice_in_dim(panel_blocks, device_id * per_device, per_device, 0)
    own_pos = lax.dynamic_slice_in_dim(panel_pos, device_id * per_device, per_device, 0)
    own_rows = own_table(x_mat, y_inv, own_panel, own_pos, block_count)
    products = lax.dot_general(
        own_rows, panel_blocks, (((1,), (1,)), ((), ())), preferred_element_type=F32
    )
    place = panel_pos % block_count * block_count + panel_pos // block_count
    position_count = block_count * block_count
    hit = jnp.arange(position_count, dtype=jnp.int32)[:, None] == place[None, :]
    row_part = jnp.sum(
        jnp.where(hit[None], products.reshape(per_device, position_count, panel_cols), 0.0), axis=1
    )
    panel_schur = lax.all_gather(row_part, ("row", "col"), axis=0, tiled=True)

    own_group = lax.dynamic_index_in_dim(group_blocks, device_id, 0, keepdims=False)
    halves = 2
    width = panel_cols // halves
    token = row_part
    local_ids = jnp.arange(sub_rows, dtype=jnp.int32)
    recv_hits = (local_ids[:, None] == recv_local.reshape(1, -1)).astype(BF16)

    def settle(rows):
        slab = jnp.dot(recv_hits, rows.reshape(-1, width), preferred_element_type=F32).astype(BF16)
        return slab, lax.all_gather(slab, "col", axis=0, tiled=True)

    received, settled = [], []
    for half in range(halves):
        cols = slice(half * width, (half + 1) * width)
        x_now, token = lax.optimization_barrier((x_mat, token))
        table = group_table(x_now, y_inv, panel_blocks[cols], panel_pos[cols], own_group, block_count)
        if half:
            settled.append(settle(received[-1]))
            table, _ = lax.optimization_barrier((table, settled[-1][0]))
        sent = send_rows(cons_blocks, table, slot_block, slot_place, places)
        token = sent
        received.append(exchange(sent.reshape(devices, capacity, width)))

    panel_schur, token = lax.optimization_barrier((panel_schur, token))
    symmetric = 0.5 * (panel_schur + panel_schur.T)
    eye = (
        lax.broadcasted_iota(jnp.int32, symmetric.shape, 0)
        == lax.broadcasted_iota(jnp.int32, symmetric.shape, 1)
    )
    diag_shift = 0.01 * jnp.sum(jnp.where(eye, symmetric, 0.0)) / panel_cols
    first = factor_start(symmetric + jnp.where(eye, diag_shift, 0.0))
    last, first = lax.optimization_barrier((received[-1], first))
    settled.append(settle(last))
    slabs, gathered = zip(*settled)
    first, token = lax.optimization_barrier((first, slabs[-1]))
    inverse = factor_end(*first)

    block_rows = trailing.shape[1] // rows_size
    slab = jnp.concatenate(slabs, axis=1)
    head = slab[: block_rows * cols_size].reshape(cols_size, block_rows, panel_cols)
    head = lax.all_to_all(head, "col", split_axis=0, concat_axis=0, tiled=True)[0]
    picked = lax.all_to_all(
        jnp.broadcast_to(head[None], (rows_size, block_rows, panel_cols)),
        "row", split_axis=0, concat_axis=0, tiled=True,
    ).reshape(rows_size * block_rows, panel_cols)

    inner = hdot(inverse, inverse, (0, 0))

    def doubled(matrix):
        rounded = lax.reduce_precision(matrix, exponent_bits=8, mantissa_bits=7)
        low = lax.reduce_precision(matrix - rounded, exponent_bits=8, mantissa_bits=7)
        return jnp.concatenate([rounded.astype(BF16), low.astype(BF16)], axis=1)

    lower_slab = lax.dot_general(
        jnp.concatenate([slab, slab], axis=1), doubled(inverse), (((1,), (1,)), ((), ())),
        preferred_element_type=F32,
    )
    weight = lax.dot_general(
        doubled(inner), jnp.concatenate([picked, picked], axis=1), (((1,), (1,)), ((), ())),
        preferred_element_type=F32,
    )
    weight = doubled(weight.T).T
    return (lower_slab, update(gathered, weight, trailing))


def solution(mesh):
    return jax.shard_map(
        body,
        mesh=mesh,
        in_specs=(
            P(),
            P(),
            P(),
            P(),
            P(),
            P(("row", "col"), None),
            P(("row", "col")),
            P(("row", "col")),
            P(("row", "col")),
            P("row", "col"),
        ),
        out_specs=(P(("row", "col"), None), P("row", "col")),
        check_vma=False,
    )
```

```python
import functools
import math

import jax
import jax.numpy as jnp
from jax import lax
from jax.experimental import pallas as pl
from jax.experimental.pallas import tpu as pltpu
from jax.sharding import PartitionSpec as P


BF16 = jnp.bfloat16
F32 = jnp.float32


def split(value):
    high = value.astype(BF16)
    low = (value - high.astype(F32)).astype(BF16)
    return high, low


def lane_half(rows, width):
    return lax.broadcasted_iota(jnp.int32, (rows, width), 1) < width // 2


def unpack_pairs(panel_ref, pairs, count, block_size):
    lanes = 2 * block_size
    keep = lane_half(count, lanes)
    for c in range(block_size // 2):
        both = panel_ref[:, c * lanes : (c + 1) * lanes].astype(F32)
        turned = pltpu.roll(both, block_size, 1)
        pitch = block_size + 1
        pairs[pl.ds(2 * c, count, stride=pitch), :] = jnp.where(keep, both, turned)
        pairs[pl.ds(2 * c + 1, count, stride=pitch), :] = jnp.where(keep, turned, both)


def column_block(ref, block, slot, block_size):
    lanes = 2 * block_size
    start = pl.multiple_of(block // 2 * lanes, lanes)
    wide = ref[:, pl.ds(start, lanes)]
    return jnp.where(block % 2 == slot, wide, pltpu.roll(wide, block_size, 1))


def group_kernel(block_count, tile, skip, pos_ref, own_ref, x_ref, y_ref, panel_ref, out_ref, left, right, pairs, scr, mid):
    step = pl.program_id(0)
    order = x_ref.shape[0]
    block_size = order // block_count
    lanes = 2 * block_size
    half = lane_half(order, lanes)

    @pl.when(step == 0)
    def _():
        for s in range(2):
            position = own_ref[s]
            a = pl.multiple_of(position // block_count * block_size, block_size)
            xa = x_ref[pl.ds(a, block_size), :]
            ya = y_ref[pl.ds(a, block_size), :]
            for p in range(block_count):
                cols = slice(p * block_size, (p + 1) * block_size)
                high, low = split(jnp.concatenate([xa[:, cols], ya[:, cols]], axis=1))
                left[p, s * block_size : (s + 1) * block_size, :] = high
                left[p, (2 + s) * block_size : (3 + s) * block_size, :] = low
        for m, ref in enumerate((y_ref, x_ref)):
            first = column_block(ref, own_ref[0] % block_count, 0, block_size)
            second = column_block(ref, own_ref[1] % block_count, 1, block_size)
            high, low = split(jnp.where(half, first, second))
            for q in range(block_count):
                rows = slice(q * block_size, (q + 1) * block_size)
                cols = slice(m * lanes, (m + 1) * lanes)
                right[q, :block_size, cols] = high[rows]
                right[q, block_size:, cols] = low[rows]

    unpack_pairs(panel_ref, pairs, tile, block_size)
    keep = lane_half(block_size, lanes)
    dot = functools.partial(jnp.dot, preferred_element_type=F32)

    def spread(j, e, t):
        position = pos_ref[skip + step * tile + j]
        p = position // block_count
        q = position % block_count
        top = dot(e, right[q])
        low_part = dot(t, right[p])
        for m, part in enumerate((top[:, :lanes], top[:, lanes:], low_part[:, :lanes], low_part[:, lanes:])):
            high, low = split(part)
            rows = slice(m * block_size, (m + 1) * block_size)
            mid[j, rows, :lanes] = high
            mid[j, rows, lanes:] = low

    def two(i, carry):
        pitch = block_size + 1
        block = jnp.concatenate(
            [pairs[pl.ds(2 * i * pitch, block_size), :], pairs[pl.ds((2 * i + 1) * pitch, block_size), :]],
            axis=0,
        )
        turned = block.T[:block_size]
        swapped = pltpu.roll(turned, block_size, 1)
        e = block.astype(BF16)
        spread(2 * i, e[:block_size], jnp.where(keep, turned, swapped).astype(BF16))
        spread(2 * i + 1, e[block_size:], jnp.where(keep, swapped, turned).astype(BF16))
        return carry

    lax.fori_loop(0, tile // 2, two, 0, unroll=tile // 2)

    def collect(j, carry):
        position = pos_ref[skip + step * tile + j]
        a = jnp.concatenate([left[position // block_count], left[position % block_count]], axis=1)
        h = dot(a, mid[j])
        b = block_size
        quad = lambda r, c: jnp.where(
            keep, h[r : r + b, c : c + lanes], h[r + b : r + 2 * b, c : c + lanes]
        )
        scr[pl.ds(j * (b + 1), b), :] = quad(0, 0) + (quad(0, lanes) + quad(2 * b, 0))
        return carry

    lax.fori_loop(0, tile, collect, 0, unroll=tile)
    keep_t = lane_half(tile, lanes)
    for r in range(0, block_size, 2):
        even = scr[pl.ds(r, tile, stride=block_size + 1), :]
        odd = scr[pl.ds(r + 1, tile, stride=block_size + 1), :]
        columns = slice(r * block_size, (r + 2) * block_size)
        out_ref[0, :, columns] = jnp.where(keep_t, even, pltpu.roll(odd, block_size, 1)).astype(BF16)
        out_ref[1, :, columns] = jnp.where(keep_t, pltpu.roll(even, block_size, 1), odd).astype(BF16)


def whole(shape):
    return pl.BlockSpec(shape, lambda *_: (0,) * len(shape))


def cost(us, count):
    return pl.CostEstimate(flops=us * 10**9, bytes_accessed=count, transcendentals=0)


def group_table(x, y, panel, positions, own, block_count, part, parts):
    width = panel.shape[1]
    count = panel.shape[0] // parts
    b = x.shape[0] // block_count
    tile = math.gcd(count, 32)
    skip = part * (count // tile)
    return pl.pallas_call(
        functools.partial(group_kernel, block_count, tile, part * count),
        grid_spec=pltpu.PrefetchScalarGridSpec(
            num_scalar_prefetch=2,
            grid=(count // tile,),
            in_specs=[
                whole(x.shape),
                whole(y.shape),
                pl.BlockSpec((tile, width), lambda i, *_: (i + skip, 0)),
            ],
            out_specs=pl.BlockSpec((2, tile, width), lambda i, *_: (0, i, 0)),
            scratch_shapes=[
                pltpu.VMEM((block_count, 4 * b, 2 * b), BF16),
                pltpu.VMEM((block_count, 2 * b, 4 * b), BF16),
                pltpu.VMEM((tile * (b + 1) + 7, 2 * b), F32),
                pltpu.VMEM((tile * (b + 1) + 7, 2 * b), F32),
                pltpu.VMEM((tile, 4 * b, 4 * b), BF16),
            ],
        ),
        out_shape=jax.ShapeDtypeStruct((2, count, width), BF16),
        cost_estimate=cost(25, 10**7),
        name="group_table",
    )(positions, own, x, y, panel)


def own_kernel(block_count, tile, pos_ref, x_ref, y_ref, panel_ref, out_ref, left, right, pairs, mid, scr):
    step = pl.program_id(0)
    order = x_ref.shape[0]
    b = order // block_count
    lanes = 2 * b
    pitch = b + 1
    positions = block_count * block_count

    @pl.when(step == 0)
    def _():
        for p in range(block_count):
            cols = slice(p * b, (p + 1) * b)
            high, low = split(jnp.concatenate([x_ref[:, cols], y_ref[:, cols]], axis=1))
            left[p, :, :lanes] = high
            left[p, :, lanes:] = low
        for m, ref in enumerate((y_ref, x_ref)):
            for q in range(block_count):
                high, low = split(ref[q * b : (q + 1) * b, :])
                cols = slice(m * order, (m + 1) * order)
                right[q, :b, cols] = high
                right[q, b:, cols] = low
        unpack_pairs(panel_ref, pairs, panel_ref.shape[0], b)

    dot = functools.partial(jnp.dot, preferred_element_type=F32)
    keep = lane_half(block_count, lanes)
    groups = order // lanes
    wide = 2 * lanes

    for j in range(tile):
        position = pos_ref[step * tile + j]
        block = pairs[pl.ds((step * tile + j) * pitch, b), :]
        turned = jnp.concatenate([block, block], axis=0).T[:b]
        top = dot(block.astype(BF16), right[position % block_count])
        low_part = dot(turned.astype(BF16), right[position // block_count])
        parts = (top[:, :order], top[:, order:], low_part[:, :order], low_part[:, order:])
        for m, part in enumerate(parts):
            high, low = split(part)
            mid[j, m * b : (m + 1) * b, :] = high
            mid[j, (4 + m) * b : (5 + m) * b, :] = low
    for j in range(tile):
        position = pos_ref[step * tile + j]
        lp, lq = left[position // block_count], left[position % block_count]
        a = jnp.concatenate([lp[:, :lanes], lq[:, :lanes]], axis=1)
        a_low = jnp.concatenate([lp[:, lanes:], lq[:, lanes:]], axis=1)
        for w in range(order // wide):
            cols = slice(w * wide, (w + 1) * wide)
            high = mid[j, : 4 * b, cols]
            h = dot(jnp.concatenate([a, a_low], axis=1), jnp.concatenate([high, high], axis=0))
            h = h + dot(a, mid[j, 4 * b :, cols])
            for g in range(wide // lanes):
                for i in range(block_count):
                    start = (((j * groups + w * (wide // lanes)) + g) * block_count + i) * pitch
                    scr[start : start + b, :] = h[i * b : (i + 1) * b, g * lanes : (g + 1) * lanes]
    for j in range(tile):
        for g in range(groups):
            base = (j * groups + g) * block_count * pitch
            first = j * positions + 2 * g * block_count
            for r in range(0, b, 2):
                even = scr[pl.ds(base + r, block_count, stride=pitch), :]
                odd = scr[pl.ds(base + r + 1, block_count, stride=pitch), :]
                one = jnp.where(keep, even, pltpu.roll(odd, b, 1))
                two = jnp.where(keep, pltpu.roll(even, b, 1), odd)
                out_ref[first : first + 2 * block_count, r * b : (r + 2) * b] = jnp.concatenate(
                    [one, two], axis=0
                ).astype(BF16)


def own_table(x, y, panel, positions, block_count):
    count, width = panel.shape
    order = x.shape[0]
    b = order // block_count
    rows = block_count * block_count
    tile = math.gcd(count, 4)
    return pl.pallas_call(
        functools.partial(own_kernel, block_count, tile),
        grid_spec=pltpu.PrefetchScalarGridSpec(
            num_scalar_prefetch=1,
            grid=(count // tile,),
            in_specs=[whole(x.shape), whole(y.shape), whole(panel.shape)],
            out_specs=pl.BlockSpec((tile * rows, width), lambda i, *_: (i, 0)),
            scratch_shapes=[
                pltpu.VMEM((block_count, order, 4 * b), BF16),
                pltpu.VMEM((block_count, 2 * b, 2 * order), BF16),
                pltpu.VMEM((max(count, 8) * (b + 1) + 7, 2 * b), F32),
                pltpu.VMEM((tile, 8 * b, order), BF16),
                pltpu.VMEM((tile * order // 2 // b * block_count * (b + 1) + 7, 2 * b), F32),
            ],
        ),
        out_shape=jax.ShapeDtypeStruct((count * rows, width), BF16),
        cost_estimate=cost(15, 10**7),
        name="own_table",
    )(positions, x, y, panel)


def row_kernel(cons_ref, table_ref, block_ref, place_ref, out_ref, total):
    step = pl.program_id(0)
    nt = (((1,), (1,)), ((), ()))
    cons = cons_ref[...]
    rows = lax.dot_general(cons, table_ref[0], nt, preferred_element_type=F32)
    block = block_ref[...]
    for s in range(1, table_ref.shape[0]):
        other = lax.dot_general(cons, table_ref[s], nt, preferred_element_type=F32)
        rows = jnp.where(block == s, other, rows)
    rows = rows.astype(BF16)
    places, tile = total.shape[0], cons.shape[0]
    hits = lax.broadcasted_iota(jnp.int32, (places, tile), 0) == place_ref[...]
    part = jnp.dot(jnp.where(hits, 1.0, 0.0).astype(BF16), rows, preferred_element_type=F32)

    @pl.when(step == 0)
    def _():
        total[...] = part

    @pl.when(step > 0)
    def _():
        total[...] += part

    @pl.when(step == pl.num_programs(0) - 1)
    def _():
        out_ref[...] = total[...].astype(BF16)


def send_rows(cons, table, block, place, places):
    slots, width = cons.shape
    cols = table.shape[1]
    tile = math.gcd(slots, 256)
    return pl.pallas_call(
        row_kernel,
        grid=(slots // tile,),
        in_specs=[
            pl.BlockSpec((tile, width), lambda i: (i, 0)),
            pl.BlockSpec(table.shape, lambda i: (0, 0, 0), pipeline_mode=pl.Buffered(1)),
            pl.BlockSpec((tile, 1), lambda i: (i, 0)),
            pl.BlockSpec((1, tile), lambda i: (0, i)),
        ],
        out_specs=whole((places, cols)),
        out_shape=jax.ShapeDtypeStruct((places, cols), BF16),
        scratch_shapes=[pltpu.VMEM((places, cols), F32)],
        cost_estimate=cost(20, 2 * 10**7),
        name="send_rows",
    )(cons, table, block, place)


def update_kernel(parts, *refs):
    row_refs, (weight_ref, trailing_ref, out_ref) = refs[:parts], refs[parts:]
    rows = jnp.concatenate([ref[...] for ref in row_refs] * 2, axis=1)
    out_ref[...] = trailing_ref[...] - jnp.dot(rows, weight_ref[...], preferred_element_type=F32)


def update(row_parts, weight, trailing):
    rows, cols = trailing.shape
    tile = math.gcd(rows, 512)
    return pl.pallas_call(
        functools.partial(update_kernel, len(row_parts)),
        grid=(rows // tile,),
        in_specs=[pl.BlockSpec((tile, part.shape[1]), lambda i: (i, 0)) for part in row_parts]
        + [whole(weight.shape), pl.BlockSpec((tile, cols), lambda i: (i, 0))],
        out_specs=pl.BlockSpec((tile, cols), lambda i: (i, 0)),
        out_shape=jax.ShapeDtypeStruct((rows, cols), F32),
        cost_estimate=cost(8, 2 * 10**7),
        name="update",
    )(*row_parts, weight, trailing)


def hdot(a, b, contract):
    return lax.dot_general(
        a, b, ((contract[:1], contract[1:]), ((), ())),
        precision=lax.Precision.HIGHEST, preferred_element_type=F32,
    )


def factor_kernel(block, begin, end, finish, *refs):
    if finish:
        s_ref, done_ref, out_ref, a, work = refs
    else:
        s_ref, a, out_ref, work = refs
    order = s_ref.shape[0]
    count = order // block
    groups = block // 8
    a[...] = s_ref[...]
    if finish:
        out_ref[...] = done_ref[...]
    row_id = lax.broadcasted_iota(jnp.int32, (8, 1), 0)
    eye = (
        lax.broadcasted_iota(jnp.int32, (block, block), 0)
        == lax.broadcasted_iota(jnp.int32, (block, block), 1)
    ).astype(F32)

    def diagonal(b, carry):
        start = pl.multiple_of(b * block, block)
        work[:, :block] = a[pl.ds(start, block), pl.ds(start, block)]
        work[:, block:] = eye
        rows = [work[8 * g : 8 * g + 8, :] for g in range(groups)]
        for k in range(block):
            g, s = divmod(k, 8)
            pivot_row = rows[g][s : s + 1, :]
            d = pivot_row[:, k : k + 1]
            inv = lax.rsqrt(d)
            inv = inv * (1.5 - 0.5 * d * inv * inv)
            scaled = pivot_row * inv
            for i in range(g, groups):
                mult = rows[i][:, k : k + 1] * inv
                if i == g:
                    mult = jnp.where(row_id > s, mult, 0.0)
                    rows[i] = jnp.where(row_id == s, scaled, rows[i] - mult * scaled)
                else:
                    rows[i] = rows[i] - mult * scaled
        inverse = jnp.concatenate([row[:, block:] for row in rows], axis=0)
        out_ref[pl.ds(start, block), pl.ds(start, block)] = inverse
        panel = hdot(a[:, pl.ds(start, block)], inverse, (1, 1))
        below = lax.broadcasted_iota(jnp.int32, (order, 1), 0) >= start + block
        panel = jnp.where(below, panel, 0.0)
        a[:, pl.ds(start, block)] = panel
        return carry, panel

    def body(b, carry):
        _, panel = diagonal(b, carry)
        start = pl.multiple_of(b * block, block)

        for i in range(1, count):
            @pl.when(b < i)
            def _():
                piece = a[i * block : (i + 1) * block, pl.ds(start, block)]
                cols = slice(i * block, (i + 1) * block)
                a[:, cols] = a[:, cols] - hdot(panel, piece, (1, 1))

        return carry

    lax.fori_loop(begin, end, body, 0)
    if not finish:
        return
    for i in range(count):
        for b in range(i + 1, count):
            out_ref[i * block : (i + 1) * block, b * block : (b + 1) * block] = jnp.zeros(
                (block, block), F32
            )
    for i in range(1, count):
        low_row = a[i * block : (i + 1) * block, : i * block]
        total = hdot(low_row, out_ref[: i * block, : i * block], (1, 0))
        own = out_ref[i * block : (i + 1) * block, i * block : (i + 1) * block]
        out_ref[i * block : (i + 1) * block, : i * block] = -hdot(own, total, (1, 0))


def factor_start(matrix):
    order = matrix.shape[0]
    block = 128
    shape = jax.ShapeDtypeStruct((order, order), F32)
    return pl.pallas_call(
        functools.partial(factor_kernel, block, 0, order // block // 2, False),
        in_specs=[pl.BlockSpec(memory_space=pltpu.VMEM)],
        out_specs=[pl.BlockSpec(memory_space=pltpu.VMEM)] * 2,
        out_shape=[shape, shape],
        scratch_shapes=[pltpu.VMEM((block, 2 * block), F32)],
        cost_estimate=cost(30, 10**6),
        name="factor_start",
    )(matrix)


def factor_end(matrix, done):
    order = matrix.shape[0]
    block = 128
    return pl.pallas_call(
        functools.partial(factor_kernel, block, order // block // 2, order // block, True),
        in_specs=[pl.BlockSpec(memory_space=pltpu.VMEM)] * 2,
        out_specs=pl.BlockSpec(memory_space=pltpu.VMEM),
        out_shape=jax.ShapeDtypeStruct((order, order), F32),
        scratch_shapes=[pltpu.VMEM((order, order), F32), pltpu.VMEM((block, 2 * block), F32)],
        cost_estimate=cost(30, 10**6),
        name="factor_end",
    )(matrix, done)


def body(
    x_mat,
    y_inv,
    panel_blocks,
    panel_pos,
    group_blocks,
    cons_blocks,
    slot_block,
    slot_row,
    group_size,
    trailing,
):
    rows_size = lax.axis_size("row")
    cols_size = lax.axis_size("col")
    devices = rows_size * cols_size
    col_index = lax.axis_index("col")
    device_id = lax.axis_index("row") * cols_size + col_index
    panel_cols = panel_blocks.shape[0]
    per_device = panel_cols // devices
    order = x_mat.shape[0]
    block_size = math.isqrt(panel_blocks.shape[1])
    block_count = order // block_size
    slot_count = cons_blocks.shape[0]

    sub_rows = trailing.shape[0] // cols_size
    base_share = sub_rows // devices
    spread = sub_rows - devices // 4 * base_share
    capacity = base_share + (spread + devices - 1) // devices
    places = devices * capacity
    slot_ids = jnp.arange(slot_count, dtype=jnp.int32)
    live_slots = slot_ids < group_size[0]
    target = slot_row // sub_rows
    dest_hits = (
        target[:, None] == jnp.arange(devices, dtype=jnp.int32)[None, :]
    ) & live_slots[:, None]
    earlier = (slot_ids[:, None] > slot_ids[None, :]).astype(BF16)
    before = jnp.dot(earlier, dest_hits.astype(BF16), preferred_element_type=F32)
    dest_rank = jnp.sum(jnp.where(dest_hits, before, 0.0), axis=1).astype(jnp.int32)
    slot_place = jnp.where(live_slots, target * capacity + dest_rank, places)
    exchange = functools.partial(
        lax.all_to_all, axis_name=("row", "col"), split_axis=0, concat_axis=0, tiled=True
    )

    own_group = lax.dynamic_index_in_dim(group_blocks, device_id, 0, keepdims=False)
    block_column, place_row = slot_block.reshape(-1, 1), slot_place.reshape(1, -1)
    halves = 2
    width = panel_cols // halves

    def half_table(half, after):
        x_now = x_mat if after is None else lax.optimization_barrier((x_mat, after))[0]
        return group_table(
            x_now, y_inv, panel_blocks, panel_pos, own_group, block_count, half, halves
        )

    def half_rows(table):
        sent = send_rows(cons_blocks, table, block_column, place_row, places)
        return sent, exchange(sent.reshape(devices, capacity, width))

    def settle(rows):
        slab = jnp.dot(recv_hits, rows.reshape(-1, width), preferred_element_type=F32).astype(BF16)
        return slab, lax.all_gather(slab, "col", axis=0, tiled=True)

    table = half_table(0, None)
    place_ids = jnp.arange(places, dtype=jnp.int32)
    tag = slot_row % sub_rows + 1
    digits = jnp.stack([tag // 32, tag % 32], axis=1).astype(BF16)
    sent_digits = jnp.dot(
        (place_ids[:, None] == slot_place[None, :]).astype(BF16), digits, preferred_element_type=F32
    ).astype(jnp.int32)
    send_local = sent_digits[:, 0] * 32 + sent_digits[:, 1] - 1
    send_local, table = lax.optimization_barrier((send_local, table))
    recv_local = exchange(send_local.reshape(devices, capacity))
    sent, early = half_rows(table)
    local_ids = jnp.arange(sub_rows, dtype=jnp.int32)
    recv_hits = (local_ids[:, None] == recv_local.reshape(1, -1)).astype(BF16)

    own_panel = lax.dynamic_slice_in_dim(panel_blocks, device_id * per_device, per_device, 0)
    own_pos = lax.dynamic_slice_in_dim(panel_pos, device_id * per_device, per_device, 0)
    own_panel, sent = lax.optimization_barrier((own_panel, sent))
    own_rows = own_table(x_mat, y_inv, own_panel, own_pos, block_count)
    products = lax.dot_general(
        own_rows, panel_blocks, (((1,), (1,)), ((), ())), preferred_element_type=F32
    )
    place = panel_pos % block_count * block_count + panel_pos // block_count
    position_count = block_count * block_count
    hit = jnp.arange(position_count, dtype=jnp.int32)[:, None] == place[None, :]
    row_part = jnp.sum(
        jnp.where(hit[None], products.reshape(per_device, position_count, panel_cols), 0.0), axis=1
    )

    def spread(part, axis, size):
        copies = jnp.broadcast_to(part[None], (size,) + part.shape)
        copies = lax.all_to_all(copies, axis, split_axis=0, concat_axis=0, tiled=True)
        return copies.reshape(-1, panel_cols)

    column_part = spread(row_part, "col", cols_size)
    early, row_part = lax.optimization_barrier((early, row_part))
    settled = [settle(early)]
    table = half_table(1, settled[0][0])
    column_part, table = lax.optimization_barrier((column_part, table))
    panel_schur = spread(column_part, "row", rows_size)
    token, late = half_rows(table)

    panel_schur, token = lax.optimization_barrier((panel_schur, token))
    symmetric = 0.5 * (panel_schur + panel_schur.T)
    eye = (
        lax.broadcasted_iota(jnp.int32, symmetric.shape, 0)
        == lax.broadcasted_iota(jnp.int32, symmetric.shape, 1)
    )
    diag_shift = 0.01 * jnp.sum(jnp.where(eye, symmetric, 0.0)) / panel_cols
    first = factor_start(symmetric + jnp.where(eye, diag_shift, 0.0))
    last, first = lax.optimization_barrier((late, first))
    settled.append(settle(last))
    slabs, gathered = zip(*settled)
    first, token = lax.optimization_barrier((first, slabs[-1]))
    inverse = factor_end(*first)

    block_rows = trailing.shape[1] // rows_size
    slab = jnp.concatenate(slabs, axis=1)
    head = slab[: block_rows * cols_size].reshape(cols_size, block_rows, panel_cols)
    head = lax.all_to_all(head, "col", split_axis=0, concat_axis=0, tiled=True)[0]
    picked = lax.all_to_all(
        jnp.broadcast_to(head[None], (rows_size, block_rows, panel_cols)),
        "row", split_axis=0, concat_axis=0, tiled=True,
    ).reshape(rows_size * block_rows, panel_cols)

    inner = hdot(inverse, inverse, (0, 0))

    def doubled(matrix):
        rounded = lax.reduce_precision(matrix, exponent_bits=8, mantissa_bits=7)
        low = lax.reduce_precision(matrix - rounded, exponent_bits=8, mantissa_bits=7)
        return jnp.concatenate([rounded.astype(BF16), low.astype(BF16)], axis=1)

    lower_slab = lax.dot_general(
        jnp.concatenate([slab, slab], axis=1), doubled(inverse), (((1,), (1,)), ((), ())),
        preferred_element_type=F32,
    )
    weight = lax.dot_general(
        doubled(inner), jnp.concatenate([picked, picked], axis=1), (((1,), (1,)), ((), ())),
        preferred_element_type=F32,
    )
    weight = doubled(weight.T).T
    return (lower_slab, update(gathered, weight, trailing))


def solution(mesh):
    return jax.shard_map(
        body,
        mesh=mesh,
        in_specs=(
            P(),
            P(),
            P(),
            P(),
            P(),
            P(("row", "col"), None),
            P(("row", "col")),
            P(("row", "col")),
            P(("row", "col")),
            P("row", "col"),
        ),
        out_specs=(P(("row", "col"), None), P("row", "col")),
        check_vma=False,
    )
```

```python
import functools
import math

import jax
import jax.numpy as jnp
from jax import lax
from jax.experimental import pallas as pl
from jax.experimental.pallas import tpu as pltpu
from jax.sharding import PartitionSpec as P


BF16 = jnp.bfloat16
F32 = jnp.float32


def split(value):
    high = value.astype(BF16)
    low = (value - high.astype(F32)).astype(BF16)
    return high, low


def lane_half(rows, width):
    return lax.broadcasted_iota(jnp.int32, (rows, width), 1) < width // 2


def unpack_pairs(panel_ref, pairs, count, block_size):
    lanes = 2 * block_size
    keep = lane_half(count, lanes)
    for c in range(block_size // 2):
        both = panel_ref[:, c * lanes : (c + 1) * lanes].astype(F32)
        turned = pltpu.roll(both, block_size, 1)
        pitch = block_size + 1
        pairs[pl.ds(2 * c, count, stride=pitch), :] = jnp.where(keep, both, turned)
        pairs[pl.ds(2 * c + 1, count, stride=pitch), :] = jnp.where(keep, turned, both)


def column_block(ref, block, slot, block_size):
    lanes = 2 * block_size
    start = pl.multiple_of(block // 2 * lanes, lanes)
    wide = ref[:, pl.ds(start, lanes)]
    return jnp.where(block % 2 == slot, wide, pltpu.roll(wide, block_size, 1))


def group_kernel(block_count, tile, skip, pos_ref, own_ref, x_ref, y_ref, panel_ref, out_ref, left, right, pairs, scr, mid):
    step = pl.program_id(0)
    order = x_ref.shape[0]
    block_size = order // block_count
    lanes = 2 * block_size
    half = lane_half(order, lanes)

    @pl.when(step == 0)
    def _():
        for s in range(2):
            position = own_ref[s]
            a = pl.multiple_of(position // block_count * block_size, block_size)
            xa = x_ref[pl.ds(a, block_size), :]
            ya = y_ref[pl.ds(a, block_size), :]
            for p in range(block_count):
                cols = slice(p * block_size, (p + 1) * block_size)
                high, low = split(jnp.concatenate([xa[:, cols], ya[:, cols]], axis=1))
                left[p, s * block_size : (s + 1) * block_size, :] = high
                left[p, (2 + s) * block_size : (3 + s) * block_size, :] = low
        for m, ref in enumerate((y_ref, x_ref)):
            first = column_block(ref, own_ref[0] % block_count, 0, block_size)
            second = column_block(ref, own_ref[1] % block_count, 1, block_size)
            high, low = split(jnp.where(half, first, second))
            for q in range(block_count):
                rows = slice(q * block_size, (q + 1) * block_size)
                cols = slice(m * lanes, (m + 1) * lanes)
                right[q, :block_size, cols] = high[rows]
                right[q, block_size:, cols] = low[rows]

    unpack_pairs(panel_ref, pairs, tile, block_size)
    keep = lane_half(block_size, lanes)
    dot = functools.partial(jnp.dot, preferred_element_type=F32)

    def spread(j, e, t):
        position = pos_ref[skip + step * tile + j]
        p = position // block_count
        q = position % block_count
        top = dot(e, right[q])
        low_part = dot(t, right[p])
        for m, part in enumerate((top[:, :lanes], top[:, lanes:], low_part[:, :lanes], low_part[:, lanes:])):
            high, low = split(part)
            rows = slice(m * block_size, (m + 1) * block_size)
            mid[j, rows, :lanes] = high
            mid[j, rows, lanes:] = low

    def two(i, carry):
        pitch = block_size + 1
        block = jnp.concatenate(
            [pairs[pl.ds(2 * i * pitch, block_size), :], pairs[pl.ds((2 * i + 1) * pitch, block_size), :]],
            axis=0,
        )
        turned = block.T[:block_size]
        swapped = pltpu.roll(turned, block_size, 1)
        e = block.astype(BF16)
        spread(2 * i, e[:block_size], jnp.where(keep, turned, swapped).astype(BF16))
        spread(2 * i + 1, e[block_size:], jnp.where(keep, swapped, turned).astype(BF16))
        return carry

    lax.fori_loop(0, tile // 2, two, 0, unroll=tile // 2)

    def collect(j, carry):
        position = pos_ref[skip + step * tile + j]
        a = jnp.concatenate([left[position // block_count], left[position % block_count]], axis=1)
        h = dot(a, mid[j])
        b = block_size
        quad = lambda r, c: jnp.where(
            keep, h[r : r + b, c : c + lanes], h[r + b : r + 2 * b, c : c + lanes]
        )
        scr[pl.ds(j * (b + 1), b), :] = quad(0, 0) + (quad(0, lanes) + quad(2 * b, 0))
        return carry

    lax.fori_loop(0, tile, collect, 0, unroll=tile)
    keep_t = lane_half(tile, lanes)
    for r in range(0, block_size, 2):
        even = scr[pl.ds(r, tile, stride=block_size + 1), :]
        odd = scr[pl.ds(r + 1, tile, stride=block_size + 1), :]
        columns = slice(r * block_size, (r + 2) * block_size)
        out_ref[0, :, columns] = jnp.where(keep_t, even, pltpu.roll(odd, block_size, 1)).astype(BF16)
        out_ref[1, :, columns] = jnp.where(keep_t, pltpu.roll(even, block_size, 1), odd).astype(BF16)


def whole(shape):
    return pl.BlockSpec(shape, lambda *_: (0,) * len(shape))


def cost(us, count):
    return pl.CostEstimate(flops=us * 10**9, bytes_accessed=count, transcendentals=0)


def group_table(x, y, panel, positions, own, block_count, part, parts):
    width = panel.shape[1]
    count = panel.shape[0] // parts
    b = x.shape[0] // block_count
    tile = math.gcd(count, 32)
    skip = part * (count // tile)
    return pl.pallas_call(
        functools.partial(group_kernel, block_count, tile, part * count),
        grid_spec=pltpu.PrefetchScalarGridSpec(
            num_scalar_prefetch=2,
            grid=(count // tile,),
            in_specs=[
                whole(x.shape),
                whole(y.shape),
                pl.BlockSpec((tile, width), lambda i, *_: (i + skip, 0)),
            ],
            out_specs=pl.BlockSpec((2, tile, width), lambda i, *_: (0, i, 0)),
            scratch_shapes=[
                pltpu.VMEM((block_count, 4 * b, 2 * b), BF16),
                pltpu.VMEM((block_count, 2 * b, 4 * b), BF16),
                pltpu.VMEM((tile * (b + 1) + 7, 2 * b), F32),
                pltpu.VMEM((tile * (b + 1) + 7, 2 * b), F32),
                pltpu.VMEM((tile, 4 * b, 4 * b), BF16),
            ],
        ),
        out_shape=jax.ShapeDtypeStruct((2, count, width), BF16),
        cost_estimate=cost(25, 10**7),
        name="group_table",
    )(positions, own, x, y, panel)


def own_kernel(block_count, tile, pos_ref, x_ref, y_ref, panel_ref, out_ref, left, right, pairs, mid, scr):
    step = pl.program_id(0)
    order = x_ref.shape[0]
    b = order // block_count
    lanes = 2 * b
    pitch = b + 1
    positions = block_count * block_count

    @pl.when(step == 0)
    def _():
        for p in range(block_count):
            cols = slice(p * b, (p + 1) * b)
            high, low = split(jnp.concatenate([x_ref[:, cols], y_ref[:, cols]], axis=1))
            left[p, :, :lanes] = high
            left[p, :, lanes:] = low
        for m, ref in enumerate((y_ref, x_ref)):
            for q in range(block_count):
                high, low = split(ref[q * b : (q + 1) * b, :])
                cols = slice(m * order, (m + 1) * order)
                right[q, :b, cols] = high
                right[q, b:, cols] = low
        unpack_pairs(panel_ref, pairs, panel_ref.shape[0], b)

    dot = functools.partial(jnp.dot, preferred_element_type=F32)
    keep = lane_half(block_count, lanes)
    groups = order // lanes
    wide = 2 * lanes

    for j in range(tile):
        position = pos_ref[step * tile + j]
        block = pairs[pl.ds((step * tile + j) * pitch, b), :]
        turned = jnp.concatenate([block, block], axis=0).T[:b]
        top = dot(block.astype(BF16), right[position % block_count])
        low_part = dot(turned.astype(BF16), right[position // block_count])
        parts = (top[:, :order], top[:, order:], low_part[:, :order], low_part[:, order:])
        for m, part in enumerate(parts):
            high, low = split(part)
            mid[j, m * b : (m + 1) * b, :] = high
            mid[j, (4 + m) * b : (5 + m) * b, :] = low
    for j in range(tile):
        position = pos_ref[step * tile + j]
        lp, lq = left[position // block_count], left[position % block_count]
        a = jnp.concatenate([lp[:, :lanes], lq[:, :lanes]], axis=1)
        a_low = jnp.concatenate([lp[:, lanes:], lq[:, lanes:]], axis=1)
        for w in range(order // wide):
            cols = slice(w * wide, (w + 1) * wide)
            high = mid[j, : 4 * b, cols]
            h = dot(jnp.concatenate([a, a_low], axis=1), jnp.concatenate([high, high], axis=0))
            h = h + dot(a, mid[j, 4 * b :, cols])
            for g in range(wide // lanes):
                for i in range(block_count):
                    start = (((j * groups + w * (wide // lanes)) + g) * block_count + i) * pitch
                    scr[start : start + b, :] = h[i * b : (i + 1) * b, g * lanes : (g + 1) * lanes]
    for j in range(tile):
        for g in range(groups):
            base = (j * groups + g) * block_count * pitch
            first = j * positions + 2 * g * block_count
            for r in range(0, b, 2):
                even = scr[pl.ds(base + r, block_count, stride=pitch), :]
                odd = scr[pl.ds(base + r + 1, block_count, stride=pitch), :]
                one = jnp.where(keep, even, pltpu.roll(odd, b, 1))
                two = jnp.where(keep, pltpu.roll(even, b, 1), odd)
                out_ref[first : first + 2 * block_count, r * b : (r + 2) * b] = jnp.concatenate(
                    [one, two], axis=0
                ).astype(BF16)


def own_table(x, y, panel, positions, block_count):
    count, width = panel.shape
    order = x.shape[0]
    b = order // block_count
    rows = block_count * block_count
    tile = math.gcd(count, 4)
    return pl.pallas_call(
        functools.partial(own_kernel, block_count, tile),
        grid_spec=pltpu.PrefetchScalarGridSpec(
            num_scalar_prefetch=1,
            grid=(count // tile,),
            in_specs=[whole(x.shape), whole(y.shape), whole(panel.shape)],
            out_specs=pl.BlockSpec((tile * rows, width), lambda i, *_: (i, 0)),
            scratch_shapes=[
                pltpu.VMEM((block_count, order, 4 * b), BF16),
                pltpu.VMEM((block_count, 2 * b, 2 * order), BF16),
                pltpu.VMEM((max(count, 8) * (b + 1) + 7, 2 * b), F32),
                pltpu.VMEM((tile, 8 * b, order), BF16),
                pltpu.VMEM((tile * order // 2 // b * block_count * (b + 1) + 7, 2 * b), F32),
            ],
        ),
        out_shape=jax.ShapeDtypeStruct((count * rows, width), BF16),
        cost_estimate=cost(15, 10**7),
        name="own_table",
    )(positions, x, y, panel)


def row_kernel(cons_ref, table_ref, block_ref, place_ref, out_ref, total):
    step = pl.program_id(0)
    nt = (((1,), (1,)), ((), ()))
    cons = cons_ref[...]
    rows = lax.dot_general(cons, table_ref[0], nt, preferred_element_type=F32)
    block = block_ref[...]
    for s in range(1, table_ref.shape[0]):
        other = lax.dot_general(cons, table_ref[s], nt, preferred_element_type=F32)
        rows = jnp.where(block == s, other, rows)
    rows = rows.astype(BF16)
    places, tile = total.shape[0], cons.shape[0]
    hits = lax.broadcasted_iota(jnp.int32, (places, tile), 0) == place_ref[...]
    part = jnp.dot(jnp.where(hits, 1.0, 0.0).astype(BF16), rows, preferred_element_type=F32)

    @pl.when(step == 0)
    def _():
        total[...] = part

    @pl.when(step > 0)
    def _():
        total[...] += part

    @pl.when(step == pl.num_programs(0) - 1)
    def _():
        out_ref[...] = total[...].astype(BF16)


def send_rows(cons, table, block, place, places):
    slots, width = cons.shape
    cols = table.shape[1]
    tile = math.gcd(slots, 256)
    return pl.pallas_call(
        row_kernel,
        grid=(slots // tile,),
        in_specs=[
            pl.BlockSpec((tile, width), lambda i: (i, 0)),
            pl.BlockSpec(table.shape, lambda i: (0, 0, 0), pipeline_mode=pl.Buffered(1)),
            pl.BlockSpec((tile, 1), lambda i: (i, 0)),
            pl.BlockSpec((1, tile), lambda i: (0, i)),
        ],
        out_specs=whole((places, cols)),
        out_shape=jax.ShapeDtypeStruct((places, cols), BF16),
        scratch_shapes=[pltpu.VMEM((places, cols), F32)],
        cost_estimate=cost(20, 2 * 10**7),
        name="send_rows",
    )(cons, table, block, place)


def update_kernel(parts, *refs):
    row_refs, (weight_ref, trailing_ref, out_ref) = refs[:parts], refs[parts:]
    rows = jnp.concatenate([ref[...] for ref in row_refs] * 2, axis=1)
    out_ref[...] = trailing_ref[...] - jnp.dot(rows, weight_ref[...], preferred_element_type=F32)


def update(row_parts, weight, trailing):
    rows, cols = trailing.shape
    tile = math.gcd(rows, 512)
    return pl.pallas_call(
        functools.partial(update_kernel, len(row_parts)),
        grid=(rows // tile,),
        in_specs=[pl.BlockSpec((tile, part.shape[1]), lambda i: (i, 0)) for part in row_parts]
        + [whole(weight.shape), pl.BlockSpec((tile, cols), lambda i: (i, 0))],
        out_specs=pl.BlockSpec((tile, cols), lambda i: (i, 0)),
        out_shape=jax.ShapeDtypeStruct((rows, cols), F32),
        cost_estimate=cost(8, 2 * 10**7),
        name="update",
    )(*row_parts, weight, trailing)


def hdot(a, b, contract):
    return lax.dot_general(
        a, b, ((contract[:1], contract[1:]), ((), ())),
        precision=lax.Precision.HIGHEST, preferred_element_type=F32,
    )


def factor_kernel(block, s_ref, out_ref, a):
    order = s_ref.shape[0]
    count = order // block
    groups = block // 8
    a[...] = s_ref[...]
    row_id = lax.broadcasted_iota(jnp.int32, (8, 1), 0)
    eye = (
        lax.broadcasted_iota(jnp.int32, (block, block), 0)
        == lax.broadcasted_iota(jnp.int32, (block, block), 1)
    ).astype(F32)

    def diagonal(b, carry):
        start = pl.multiple_of(b * block, block)
        tile = (8, block)
        left = [a[pl.ds(start + 8 * g, 8), pl.ds(start, block)] for g in range(groups)]
        right = [eye[8 * g : 8 * g + 8, :] for g in range(groups)]
        for g in range(groups):
            spot = lambda i, s, t: jnp.broadcast_to(
                left[i][s : s + 1, 8 * g + t : 8 * g + t + 1], tile
            )
            d = {(s, t): spot(g, s, t) for t in range(8) for s in range(t, 8)}
            inv, low, scaled = [], {}, []
            heads = [
                [jnp.broadcast_to(side[g][t : t + 1, :], tile) for side in (left, right)]
                for t in range(8)
            ]
            for t in range(8):
                root = lax.rsqrt(d[t, t])
                root = root * (1.5 - 0.5 * d[t, t] * root * root)
                inv.append(root)
                for s in range(t + 1, 8):
                    low[s, t] = d[s, t] * root
                for u in range(t + 1, 8):
                    for s in range(u, 8):
                        d[s, u] = d[s, u] - low[s, t] * low[u, t]
                now = heads[t]
                for u in range(t):
                    now = [n - low[t, u] * r for n, r in zip(now, scaled[u])]
                scaled.append([n * root for n in now])
            for i in range(g + 1, groups):
                mult = []
                for t in range(8):
                    m = jnp.broadcast_to(left[i][:, 8 * g + t : 8 * g + t + 1], tile)
                    for u in range(t):
                        m = m - mult[u] * low[t, u]
                    mult.append(m * inv[t])
                for t in range(8):
                    left[i] = left[i] - mult[t] * scaled[t][0]
                    right[i] = right[i] - mult[t] * scaled[t][1]
            done = scaled[0][1]
            for t in range(1, 8):
                done = jnp.where(row_id == t, scaled[t][1], done)
            right[g] = done
        inverse = jnp.concatenate(right, axis=0)
        out_ref[pl.ds(start, block), pl.ds(start, block)] = inverse
        panel = hdot(a[:, pl.ds(start, block)], inverse, (1, 1))
        below = lax.broadcasted_iota(jnp.int32, (order, 1), 0) >= start + block
        panel = jnp.where(below, panel, 0.0)
        a[:, pl.ds(start, block)] = panel
        return carry, panel

    def body(b, carry):
        _, panel = diagonal(b, carry)
        start = pl.multiple_of(b * block, block)

        for i in range(1, count):
            @pl.when(b < i)
            def _():
                piece = a[i * block : (i + 1) * block, pl.ds(start, block)]
                cols = slice(i * block, (i + 1) * block)
                a[:, cols] = a[:, cols] - hdot(panel, piece, (1, 1))

        return carry

    lax.fori_loop(0, count, body, 0)
    for i in range(count):
        for b in range(i + 1, count):
            out_ref[i * block : (i + 1) * block, b * block : (b + 1) * block] = jnp.zeros(
                (block, block), F32
            )
    for i in range(1, count):
        low_row = a[i * block : (i + 1) * block, : i * block]
        total = hdot(low_row, out_ref[: i * block, : i * block], (1, 0))
        own = out_ref[i * block : (i + 1) * block, i * block : (i + 1) * block]
        out_ref[i * block : (i + 1) * block, : i * block] = -hdot(own, total, (1, 0))


def inverse_factor(matrix):
    order = matrix.shape[0]
    block = 128
    return pl.pallas_call(
        functools.partial(factor_kernel, block),
        in_specs=[pl.BlockSpec(memory_space=pltpu.VMEM)],
        out_specs=pl.BlockSpec(memory_space=pltpu.VMEM),
        out_shape=jax.ShapeDtypeStruct((order, order), F32),
        scratch_shapes=[pltpu.VMEM((order, order), F32)],
        cost_estimate=cost(30, 10**6),
        name="inverse_factor",
    )(matrix)


def body(
    x_mat,
    y_inv,
    panel_blocks,
    panel_pos,
    group_blocks,
    cons_blocks,
    slot_block,
    slot_row,
    group_size,
    trailing,
):
    rows_size = lax.axis_size("row")
    cols_size = lax.axis_size("col")
    devices = rows_size * cols_size
    col_index = lax.axis_index("col")
    device_id = lax.axis_index("row") * cols_size + col_index
    panel_cols = panel_blocks.shape[0]
    per_device = panel_cols // devices
    order = x_mat.shape[0]
    block_size = math.isqrt(panel_blocks.shape[1])
    block_count = order // block_size
    slot_count = cons_blocks.shape[0]

    sub_rows = trailing.shape[0] // cols_size
    base_share = sub_rows // devices
    spread = sub_rows - devices // 4 * base_share
    capacity = base_share + (spread + devices - 1) // devices
    places = devices * capacity
    slot_ids = jnp.arange(slot_count, dtype=jnp.int32)
    live_slots = slot_ids < group_size[0]
    target = slot_row // sub_rows
    dest_hits = (
        target[:, None] == jnp.arange(devices, dtype=jnp.int32)[None, :]
    ) & live_slots[:, None]
    earlier = (slot_ids[:, None] > slot_ids[None, :]).astype(BF16)
    before = jnp.dot(earlier, dest_hits.astype(BF16), preferred_element_type=F32)
    dest_rank = jnp.sum(jnp.where(dest_hits, before, 0.0), axis=1).astype(jnp.int32)
    slot_place = jnp.where(live_slots, target * capacity + dest_rank, places)
    exchange = functools.partial(
        lax.all_to_all, axis_name=("row", "col"), split_axis=0, concat_axis=0, tiled=True
    )

    own_group = lax.dynamic_index_in_dim(group_blocks, device_id, 0, keepdims=False)
    block_column, place_row = slot_block.reshape(-1, 1), slot_place.reshape(1, -1)
    halves = 2
    width = panel_cols // halves

    def half_table(half, after):
        x_now = x_mat if after is None else lax.optimization_barrier((x_mat, after))[0]
        return group_table(
            x_now, y_inv, panel_blocks, panel_pos, own_group, block_count, half, halves
        )

    def half_rows(table):
        sent = send_rows(cons_blocks, table, block_column, place_row, places)
        return sent, exchange(sent.reshape(devices, capacity, width))

    def settle(rows):
        slab = jnp.dot(recv_hits, rows.reshape(-1, width), preferred_element_type=F32).astype(BF16)
        return slab, lax.all_gather(slab, "col", axis=0, tiled=True)

    place_ids = jnp.arange(places, dtype=jnp.int32)
    tag = slot_row % sub_rows + 1
    digits = jnp.stack([tag // 32, tag % 32], axis=1).astype(BF16)
    sent_digits = jnp.dot(
        (place_ids[:, None] == slot_place[None, :]).astype(BF16), digits, preferred_element_type=F32
    )
    send_local = sent_digits[:, 0] * 32 + sent_digits[:, 1] - 1
    padded = jnp.pad(send_local, (0, 16 * panel_cols - places)).reshape(16, panel_cols)
    tags = lax.all_gather(padded, ("row", "col"), axis=0, tiled=True)
    recv_local = lax.dynamic_index_in_dim(
        tags.reshape(devices, -1)[:, :places].reshape(devices, devices, capacity),
        device_id, 1, keepdims=False,
    ).astype(jnp.int32)
    local_ids = jnp.arange(sub_rows, dtype=jnp.int32)
    recv_hits = (local_ids[:, None] == recv_local.reshape(1, -1)).astype(BF16)

    sent, early = half_rows(half_table(0, None))
    table = half_table(1, sent)
    early, table = lax.optimization_barrier((early, table))
    first_slab, first_rows = settle(early)
    table, first_slab = lax.optimization_barrier((table, first_slab))
    sent, late = half_rows(table)

    own_panel = lax.dynamic_slice_in_dim(panel_blocks, device_id * per_device, per_device, 0)
    own_pos = lax.dynamic_slice_in_dim(panel_pos, device_id * per_device, per_device, 0)
    own_panel, sent = lax.optimization_barrier((own_panel, sent))
    own_rows = own_table(x_mat, y_inv, own_panel, own_pos, block_count)
    products = lax.dot_general(
        own_rows, panel_blocks, (((1,), (1,)), ((), ())), preferred_element_type=F32
    )
    place = panel_pos % block_count * block_count + panel_pos // block_count
    position_count = block_count * block_count
    hit = jnp.arange(position_count, dtype=jnp.int32)[:, None] == place[None, :]
    row_part = jnp.sum(
        jnp.where(hit[None], products.reshape(per_device, position_count, panel_cols), 0.0), axis=1
    )

    def spread(part, axis, size):
        copies = jnp.broadcast_to(part[None], (size,) + part.shape)
        copies = lax.all_to_all(copies, axis, split_axis=0, concat_axis=0, tiled=True)
        return copies.reshape(-1, panel_cols)

    late, row_part = lax.optimization_barrier((late, row_part))
    column_part = spread(row_part, "col", cols_size)
    last_slab, last_rows = settle(late)
    panel_schur = spread(column_part, "row", rows_size)

    block_rows = trailing.shape[1] // rows_size
    slab = jnp.concatenate([first_slab, last_slab], axis=1)
    head = slab[: block_rows * cols_size].reshape(cols_size, block_rows, panel_cols)
    head, panel_schur = lax.optimization_barrier((head, panel_schur))
    head = lax.all_to_all(head, "col", split_axis=0, concat_axis=0, tiled=True)[0]
    picked = spread(head, "row", rows_size)

    symmetric = 0.5 * (panel_schur + panel_schur.T)
    eye = (
        lax.broadcasted_iota(jnp.int32, symmetric.shape, 0)
        == lax.broadcasted_iota(jnp.int32, symmetric.shape, 1)
    )
    diag_shift = 0.01 * jnp.sum(jnp.where(eye, symmetric, 0.0)) / panel_cols
    inverse = inverse_factor(symmetric + jnp.where(eye, diag_shift, 0.0))
    inner = hdot(inverse, inverse, (0, 0))

    def doubled(matrix):
        rounded = lax.reduce_precision(matrix, exponent_bits=8, mantissa_bits=7)
        low = lax.reduce_precision(matrix - rounded, exponent_bits=8, mantissa_bits=7)
        return jnp.concatenate([rounded.astype(BF16), low.astype(BF16)], axis=1)

    lower_slab = lax.dot_general(
        jnp.concatenate([slab, slab], axis=1), doubled(inverse), (((1,), (1,)), ((), ())),
        preferred_element_type=F32,
    )
    weight = lax.dot_general(
        doubled(inner), jnp.concatenate([picked, picked], axis=1), (((1,), (1,)), ((), ())),
        preferred_element_type=F32,
    )
    weight = doubled(weight.T).T
    return (lower_slab, update([first_rows, last_rows], weight, trailing))


def solution(mesh):
    return jax.shard_map(
        body,
        mesh=mesh,
        in_specs=(
            P(),
            P(),
            P(),
            P(),
            P(),
            P(("row", "col"), None),
            P(("row", "col")),
            P(("row", "col")),
            P(("row", "col")),
            P("row", "col"),
        ),
        out_specs=(P(("row", "col"), None), P("row", "col")),
        check_vma=False,
    )
```

```python
import functools
import math

import jax
import jax.numpy as jnp
from jax import lax
from jax.experimental import pallas as pl
from jax.experimental.pallas import tpu as pltpu
from jax.sharding import PartitionSpec as P


BF16 = jnp.bfloat16
F32 = jnp.float32


def split(value):
    high = value.astype(BF16)
    low = (value - high.astype(F32)).astype(BF16)
    return high, low


def lane_half(rows, width):
    return lax.broadcasted_iota(jnp.int32, (rows, width), 1) < width // 2


def unpack_pairs(panel_ref, pairs, count, block_size):
    lanes = 2 * block_size
    keep = lane_half(count, lanes)
    for c in range(block_size // 2):
        both = panel_ref[:, c * lanes : (c + 1) * lanes].astype(F32)
        turned = pltpu.roll(both, block_size, 1)
        pitch = block_size + 1
        pairs[pl.ds(2 * c, count, stride=pitch), :] = jnp.where(keep, both, turned)
        pairs[pl.ds(2 * c + 1, count, stride=pitch), :] = jnp.where(keep, turned, both)


def column_block(ref, block, slot, block_size):
    lanes = 2 * block_size
    start = pl.multiple_of(block // 2 * lanes, lanes)
    wide = ref[:, pl.ds(start, lanes)]
    return jnp.where(block % 2 == slot, wide, pltpu.roll(wide, block_size, 1))


def group_kernel(block_count, tile, skip, pos_ref, own_ref, x_ref, y_ref, panel_ref, out_ref, left, right, pairs, scr, mid):
    step = pl.program_id(0)
    order = x_ref.shape[0]
    block_size = order // block_count
    lanes = 2 * block_size
    half = lane_half(order, lanes)

    @pl.when(step == 0)
    def _():
        for s in range(2):
            position = own_ref[s]
            a = pl.multiple_of(position // block_count * block_size, block_size)
            xa = x_ref[pl.ds(a, block_size), :]
            ya = y_ref[pl.ds(a, block_size), :]
            for p in range(block_count):
                cols = slice(p * block_size, (p + 1) * block_size)
                high, low = split(jnp.concatenate([xa[:, cols], ya[:, cols]], axis=1))
                left[p, s * block_size : (s + 1) * block_size, :] = high
                left[p, (2 + s) * block_size : (3 + s) * block_size, :] = low
        for m, ref in enumerate((y_ref, x_ref)):
            first = column_block(ref, own_ref[0] % block_count, 0, block_size)
            second = column_block(ref, own_ref[1] % block_count, 1, block_size)
            high, low = split(jnp.where(half, first, second))
            for q in range(block_count):
                rows = slice(q * block_size, (q + 1) * block_size)
                cols = slice(m * lanes, (m + 1) * lanes)
                right[q, :block_size, cols] = high[rows]
                right[q, block_size:, cols] = low[rows]

    unpack_pairs(panel_ref, pairs, tile, block_size)
    keep = lane_half(block_size, lanes)
    dot = functools.partial(jnp.dot, preferred_element_type=F32)

    def spread(j, e, t):
        position = pos_ref[skip + step * tile + j]
        p = position // block_count
        q = position % block_count
        top = dot(e, right[q])
        low_part = dot(t, right[p])
        for m, part in enumerate((top[:, :lanes], top[:, lanes:], low_part[:, :lanes], low_part[:, lanes:])):
            high, low = split(part)
            rows = slice(m * block_size, (m + 1) * block_size)
            mid[j, rows, :lanes] = high
            mid[j, rows, lanes:] = low

    def two(i, carry):
        pitch = block_size + 1
        block = jnp.concatenate(
            [pairs[pl.ds(2 * i * pitch, block_size), :], pairs[pl.ds((2 * i + 1) * pitch, block_size), :]],
            axis=0,
        )
        turned = block.T[:block_size]
        swapped = pltpu.roll(turned, block_size, 1)
        e = block.astype(BF16)
        spread(2 * i, e[:block_size], jnp.where(keep, turned, swapped).astype(BF16))
        spread(2 * i + 1, e[block_size:], jnp.where(keep, swapped, turned).astype(BF16))
        return carry

    lax.fori_loop(0, tile // 2, two, 0, unroll=tile // 2)

    def collect(j, carry):
        position = pos_ref[skip + step * tile + j]
        a = jnp.concatenate([left[position // block_count], left[position % block_count]], axis=1)
        h = dot(a, mid[j])
        b = block_size
        quad = lambda r, c: jnp.where(
            keep, h[r : r + b, c : c + lanes], h[r + b : r + 2 * b, c : c + lanes]
        )
        scr[pl.ds(j * (b + 1), b), :] = quad(0, 0) + (quad(0, lanes) + quad(2 * b, 0))
        return carry

    lax.fori_loop(0, tile, collect, 0, unroll=tile)
    keep_t = lane_half(tile, lanes)
    for r in range(0, block_size, 2):
        even = scr[pl.ds(r, tile, stride=block_size + 1), :]
        odd = scr[pl.ds(r + 1, tile, stride=block_size + 1), :]
        columns = slice(r * block_size, (r + 2) * block_size)
        out_ref[0, :, columns] = jnp.where(keep_t, even, pltpu.roll(odd, block_size, 1)).astype(BF16)
        out_ref[1, :, columns] = jnp.where(keep_t, pltpu.roll(even, block_size, 1), odd).astype(BF16)


def whole(shape):
    return pl.BlockSpec(shape, lambda *_: (0,) * len(shape))


def cost(us, count):
    return pl.CostEstimate(flops=us * 10**9, bytes_accessed=count, transcendentals=0)


def group_table(x, y, panel, positions, own, block_count, part, parts):
    width = panel.shape[1]
    count = panel.shape[0] // parts
    b = x.shape[0] // block_count
    tile = math.gcd(count, 32)
    skip = part * (count // tile)
    return pl.pallas_call(
        functools.partial(group_kernel, block_count, tile, part * count),
        grid_spec=pltpu.PrefetchScalarGridSpec(
            num_scalar_prefetch=2,
            grid=(count // tile,),
            in_specs=[
                whole(x.shape),
                whole(y.shape),
                pl.BlockSpec((tile, width), lambda i, *_: (i + skip, 0)),
            ],
            out_specs=pl.BlockSpec((2, tile, width), lambda i, *_: (0, i, 0)),
            scratch_shapes=[
                pltpu.VMEM((block_count, 4 * b, 2 * b), BF16),
                pltpu.VMEM((block_count, 2 * b, 4 * b), BF16),
                pltpu.VMEM((tile * (b + 1) + 7, 2 * b), F32),
                pltpu.VMEM((tile * (b + 1) + 7, 2 * b), F32),
                pltpu.VMEM((tile, 4 * b, 4 * b), BF16),
            ],
        ),
        out_shape=jax.ShapeDtypeStruct((2, count, width), BF16),
        cost_estimate=cost(25, 10**7),
        name="group_table",
    )(positions, own, x, y, panel)


def own_kernel(
    block_count, tile, pos_ref, x_ref, y_ref, panel_ref, all_ref, place_ref, out_ref, left, right, pairs, mid, scr, table
):
    step = pl.program_id(0)
    order = x_ref.shape[0]
    b = order // block_count
    lanes = 2 * b
    pitch = b + 1
    positions = block_count * block_count

    @pl.when(step == 0)
    def _():
        for p in range(block_count):
            cols = slice(p * b, (p + 1) * b)
            high, low = split(jnp.concatenate([x_ref[:, cols], y_ref[:, cols]], axis=1))
            left[p, :, :lanes] = high
            left[p, :, lanes:] = low
        for m, ref in enumerate((y_ref, x_ref)):
            for q in range(block_count):
                high, low = split(ref[q * b : (q + 1) * b, :])
                cols = slice(m * order, (m + 1) * order)
                right[q, :b, cols] = high
                right[q, b:, cols] = low
        unpack_pairs(panel_ref, pairs, panel_ref.shape[0], b)

    dot = functools.partial(jnp.dot, preferred_element_type=F32)
    keep = lane_half(block_count, lanes)
    groups = order // lanes
    wide = 2 * lanes

    for j in range(tile):
        position = pos_ref[step * tile + j]
        block = pairs[pl.ds((step * tile + j) * pitch, b), :]
        turned = jnp.concatenate([block, block], axis=0).T[:b]
        top = dot(block.astype(BF16), right[position % block_count])
        low_part = dot(turned.astype(BF16), right[position // block_count])
        parts = (top[:, :order], top[:, order:], low_part[:, :order], low_part[:, order:])
        for m, part in enumerate(parts):
            high, low = split(part)
            mid[j, m * b : (m + 1) * b, :] = high
            mid[j, (4 + m) * b : (5 + m) * b, :] = low
    for j in range(tile):
        position = pos_ref[step * tile + j]
        lp, lq = left[position // block_count], left[position % block_count]
        a = jnp.concatenate([lp[:, :lanes], lq[:, :lanes]], axis=1)
        a_low = jnp.concatenate([lp[:, lanes:], lq[:, lanes:]], axis=1)
        for w in range(order // wide):
            cols = slice(w * wide, (w + 1) * wide)
            high = mid[j, : 4 * b, cols]
            h = dot(jnp.concatenate([a, a_low], axis=1), jnp.concatenate([high, high], axis=0))
            h = h + dot(a, mid[j, 4 * b :, cols])
            for g in range(wide // lanes):
                for i in range(block_count):
                    start = (((j * groups + w * (wide // lanes)) + g) * block_count + i) * pitch
                    scr[start : start + b, :] = h[i * b : (i + 1) * b, g * lanes : (g + 1) * lanes]
    for j in range(tile):
        for g in range(groups):
            base = (j * groups + g) * block_count * pitch
            first = j * positions + 2 * g * block_count
            for r in range(0, b, 2):
                even = scr[pl.ds(base + r, block_count, stride=pitch), :]
                odd = scr[pl.ds(base + r + 1, block_count, stride=pitch), :]
                one = jnp.where(keep, even, pltpu.roll(odd, b, 1))
                two = jnp.where(keep, pltpu.roll(even, b, 1), odd)
                table[first : first + 2 * block_count, r * b : (r + 2) * b] = jnp.concatenate(
                    [one, two], axis=0
                ).astype(BF16)
    products = lax.dot_general(
        table[...], all_ref[...], (((1,), (1,)), ((), ())), preferred_element_type=F32
    )
    hit = (
        lax.broadcasted_iota(jnp.int32, (positions, products.shape[1]), 0) == place_ref[...]
    )
    for j in range(tile):
        part = jnp.where(hit, products[j * positions : (j + 1) * positions], 0.0)
        out_ref[pl.ds(step * tile + j, 1), :] = jnp.sum(part, axis=0, keepdims=True)


def own_part(x, y, panel, positions, everything, place, block_count):
    count, width = panel.shape
    columns = everything.shape[0]
    order = x.shape[0]
    b = order // block_count
    rows = block_count * block_count
    tile = math.gcd(count, 4)
    return pl.pallas_call(
        functools.partial(own_kernel, block_count, tile),
        grid_spec=pltpu.PrefetchScalarGridSpec(
            num_scalar_prefetch=1,
            grid=(count // tile,),
            in_specs=[
                whole(x.shape),
                whole(y.shape),
                whole(panel.shape),
                pl.BlockSpec(everything.shape, lambda *_: (0, 0), pipeline_mode=pl.Buffered(1)),
                whole(place.shape),
            ],
            out_specs=whole((count, columns)),
            scratch_shapes=[
                pltpu.VMEM((block_count, order, 4 * b), BF16),
                pltpu.VMEM((block_count, 2 * b, 2 * order), BF16),
                pltpu.VMEM((max(count, 8) * (b + 1) + 7, 2 * b), F32),
                pltpu.VMEM((tile, 8 * b, order), BF16),
                pltpu.VMEM((tile * order // 2 // b * block_count * (b + 1) + 7, 2 * b), F32),
                pltpu.VMEM((tile * rows, width), BF16),
            ],
        ),
        out_shape=jax.ShapeDtypeStruct((count, columns), F32),
        cost_estimate=cost(22, 10**7),
        name="own_part",
    )(positions, x, y, panel, everything, place)


def row_kernel(cons_ref, table_ref, block_ref, place_ref, out_ref, total):
    step = pl.program_id(0)
    nt = (((1,), (1,)), ((), ()))
    cons = cons_ref[...]
    rows = lax.dot_general(cons, table_ref[0], nt, preferred_element_type=F32)
    block = block_ref[...]
    for s in range(1, table_ref.shape[0]):
        other = lax.dot_general(cons, table_ref[s], nt, preferred_element_type=F32)
        rows = jnp.where(block == s, other, rows)
    rows = rows.astype(BF16)
    places, tile = total.shape[0], cons.shape[0]
    hits = lax.broadcasted_iota(jnp.int32, (places, tile), 0) == place_ref[...]
    part = jnp.dot(jnp.where(hits, 1.0, 0.0).astype(BF16), rows, preferred_element_type=F32)

    @pl.when(step == 0)
    def _():
        total[...] = part

    @pl.when(step > 0)
    def _():
        total[...] += part

    @pl.when(step == pl.num_programs(0) - 1)
    def _():
        out_ref[...] = total[...].astype(BF16)


def send_rows(cons, table, block, place, places):
    slots, width = cons.shape
    cols = table.shape[1]
    tile = math.gcd(slots, 256)
    return pl.pallas_call(
        row_kernel,
        grid=(slots // tile,),
        in_specs=[
            pl.BlockSpec((tile, width), lambda i: (i, 0)),
            pl.BlockSpec(table.shape, lambda i: (0, 0, 0), pipeline_mode=pl.Buffered(1)),
            pl.BlockSpec((tile, 1), lambda i: (i, 0)),
            pl.BlockSpec((1, tile), lambda i: (0, i)),
        ],
        out_specs=whole((places, cols)),
        out_shape=jax.ShapeDtypeStruct((places, cols), BF16),
        scratch_shapes=[pltpu.VMEM((places, cols), F32)],
        cost_estimate=cost(20, 2 * 10**7),
        name="send_rows",
    )(cons, table, block, place)


def update_kernel(parts, *refs):
    row_refs, (weight_ref, trailing_ref, out_ref) = refs[:parts], refs[parts:]
    rows = jnp.concatenate([ref[...] for ref in row_refs] * 2, axis=1)
    out_ref[...] = trailing_ref[...] - jnp.dot(rows, weight_ref[...], preferred_element_type=F32)


def update(row_parts, weight, trailing):
    rows, cols = trailing.shape
    tile = math.gcd(rows, 512)
    return pl.pallas_call(
        functools.partial(update_kernel, len(row_parts)),
        grid=(rows // tile,),
        in_specs=[pl.BlockSpec((tile, part.shape[1]), lambda i: (i, 0)) for part in row_parts]
        + [whole(weight.shape), pl.BlockSpec((tile, cols), lambda i: (i, 0))],
        out_specs=pl.BlockSpec((tile, cols), lambda i: (i, 0)),
        out_shape=jax.ShapeDtypeStruct((rows, cols), F32),
        cost_estimate=cost(8, 2 * 10**7),
        name="update",
    )(*row_parts, weight, trailing)


def hdot(a, b, contract):
    return lax.dot_general(
        a, b, ((contract[:1], contract[1:]), ((), ())),
        precision=lax.Precision.HIGHEST, preferred_element_type=F32,
    )


def factor_kernel(block, s_ref, out_ref, a):
    order = s_ref.shape[0]
    count = order // block
    groups = block // 8
    a[...] = s_ref[...]
    row_id = lax.broadcasted_iota(jnp.int32, (8, 1), 0)
    eye = (
        lax.broadcasted_iota(jnp.int32, (block, block), 0)
        == lax.broadcasted_iota(jnp.int32, (block, block), 1)
    ).astype(F32)

    def diagonal(b, carry):
        start = pl.multiple_of(b * block, block)
        tile = (8, block)
        left = [a[pl.ds(start + 8 * g, 8), pl.ds(start, block)] for g in range(groups)]
        right = [eye[8 * g : 8 * g + 8, :] for g in range(groups)]
        for g in range(groups):
            spot = lambda i, s, t: jnp.broadcast_to(
                left[i][s : s + 1, 8 * g + t : 8 * g + t + 1], tile
            )
            d = {(s, t): spot(g, s, t) for t in range(8) for s in range(t, 8)}
            inv, low, scaled = [], {}, []
            heads = [
                [jnp.broadcast_to(side[g][t : t + 1, :], tile) for side in (left, right)]
                for t in range(8)
            ]
            for t in range(8):
                root = lax.rsqrt(d[t, t])
                root = root * (1.5 - 0.5 * d[t, t] * root * root)
                inv.append(root)
                for s in range(t + 1, 8):
                    low[s, t] = d[s, t] * root
                for u in range(t + 1, 8):
                    for s in range(u, 8):
                        d[s, u] = d[s, u] - low[s, t] * low[u, t]
                now = heads[t]
                for u in range(t):
                    now = [n - low[t, u] * r for n, r in zip(now, scaled[u])]
                scaled.append([n * root for n in now])
            for i in range(g + 1, groups):
                mult = []
                for t in range(8):
                    m = jnp.broadcast_to(left[i][:, 8 * g + t : 8 * g + t + 1], tile)
                    for u in range(t):
                        m = m - mult[u] * low[t, u]
                    mult.append(m * inv[t])
                for t in range(8):
                    left[i] = left[i] - mult[t] * scaled[t][0]
                    right[i] = right[i] - mult[t] * scaled[t][1]
            done = scaled[0][1]
            for t in range(1, 8):
                done = jnp.where(row_id == t, scaled[t][1], done)
            right[g] = done
        inverse = jnp.concatenate(right, axis=0)
        out_ref[pl.ds(start, block), pl.ds(start, block)] = inverse
        panel = hdot(a[:, pl.ds(start, block)], inverse, (1, 1))
        below = lax.broadcasted_iota(jnp.int32, (order, 1), 0) >= start + block
        panel = jnp.where(below, panel, 0.0)
        a[:, pl.ds(start, block)] = panel
        return carry, panel

    def body(b, carry):
        _, panel = diagonal(b, carry)
        start = pl.multiple_of(b * block, block)

        for i in range(1, count):
            @pl.when(b < i)
            def _():
                piece = a[i * block : (i + 1) * block, pl.ds(start, block)]
                cols = slice(i * block, (i + 1) * block)
                a[:, cols] = a[:, cols] - hdot(panel, piece, (1, 1))

        return carry

    lax.fori_loop(0, count, body, 0)
    for i in range(count):
        for b in range(i + 1, count):
            out_ref[i * block : (i + 1) * block, b * block : (b + 1) * block] = jnp.zeros(
                (block, block), F32
            )
    for i in range(1, count):
        low_row = a[i * block : (i + 1) * block, : i * block]
        total = hdot(low_row, out_ref[: i * block, : i * block], (1, 0))
        own = out_ref[i * block : (i + 1) * block, i * block : (i + 1) * block]
        out_ref[i * block : (i + 1) * block, : i * block] = -hdot(own, total, (1, 0))


def inverse_factor(matrix):
    order = matrix.shape[0]
    block = 128
    return pl.pallas_call(
        functools.partial(factor_kernel, block),
        in_specs=[pl.BlockSpec(memory_space=pltpu.VMEM)],
        out_specs=pl.BlockSpec(memory_space=pltpu.VMEM),
        out_shape=jax.ShapeDtypeStruct((order, order), F32),
        scratch_shapes=[pltpu.VMEM((order, order), F32)],
        cost_estimate=cost(30, 10**6),
        name="inverse_factor",
    )(matrix)


def body(
    x_mat,
    y_inv,
    panel_blocks,
    panel_pos,
    group_blocks,
    cons_blocks,
    slot_block,
    slot_row,
    group_size,
    trailing,
):
    rows_size = lax.axis_size("row")
    cols_size = lax.axis_size("col")
    devices = rows_size * cols_size
    col_index = lax.axis_index("col")
    device_id = lax.axis_index("row") * cols_size + col_index
    panel_cols = panel_blocks.shape[0]
    per_device = panel_cols // devices
    order = x_mat.shape[0]
    block_size = math.isqrt(panel_blocks.shape[1])
    block_count = order // block_size
    slot_count = cons_blocks.shape[0]

    sub_rows = trailing.shape[0] // cols_size
    base_share = sub_rows // devices
    spread = sub_rows - devices // 4 * base_share
    capacity = base_share + (spread + devices - 1) // devices
    places = devices * capacity
    slot_ids = jnp.arange(slot_count, dtype=jnp.int32)
    live_slots = slot_ids < group_size[0]
    target = slot_row // sub_rows
    dest_hits = (
        target[:, None] == jnp.arange(devices, dtype=jnp.int32)[None, :]
    ) & live_slots[:, None]
    earlier = (slot_ids[:, None] > slot_ids[None, :]).astype(BF16)
    before = jnp.dot(earlier, dest_hits.astype(BF16), preferred_element_type=F32)
    dest_rank = jnp.sum(jnp.where(dest_hits, before, 0.0), axis=1).astype(jnp.int32)
    slot_place = jnp.where(live_slots, target * capacity + dest_rank, places)
    exchange = functools.partial(
        lax.all_to_all, axis_name=("row", "col"), split_axis=0, concat_axis=0, tiled=True
    )

    own_group = lax.dynamic_index_in_dim(group_blocks, device_id, 0, keepdims=False)
    block_column, place_row = slot_block.reshape(-1, 1), slot_place.reshape(1, -1)
    halves = 2
    width = panel_cols // halves

    def half_table(half, after):
        x_now = x_mat if after is None else lax.optimization_barrier((x_mat, after))[0]
        return group_table(
            x_now, y_inv, panel_blocks, panel_pos, own_group, block_count, half, halves
        )

    def half_rows(table):
        sent = send_rows(cons_blocks, table, block_column, place_row, places)
        return sent, exchange(sent.reshape(devices, capacity, width))

    def settle(rows):
        slab = jnp.dot(recv_hits, rows.reshape(-1, width), preferred_element_type=F32).astype(BF16)
        return slab, lax.all_gather(slab, "col", axis=0, tiled=True)

    place_ids = jnp.arange(places, dtype=jnp.int32)
    tag = slot_row % sub_rows + 1
    arriving = place_ids[:, None] == slot_place[None, :]
    send_local = jnp.sum(jnp.where(arriving, tag[None, :], 0), axis=1).astype(F32) - 1.0
    padded = jnp.pad(send_local, (0, 16 * panel_cols - places)).reshape(16, panel_cols)
    tags = lax.all_gather(padded, ("row", "col"), axis=0, tiled=True)
    recv_local = lax.dynamic_index_in_dim(
        tags.reshape(devices, -1)[:, :places].reshape(devices, devices, capacity),
        device_id, 1, keepdims=False,
    ).astype(jnp.int32)
    local_ids = jnp.arange(sub_rows, dtype=jnp.int32)
    recv_hits = (local_ids[:, None] == recv_local.reshape(1, -1)).astype(BF16)

    def spread(part, axis, size):
        copies = jnp.broadcast_to(part[None], (size,) + part.shape)
        copies = lax.all_to_all(copies, axis, split_axis=0, concat_axis=0, tiled=True)
        return copies.reshape(-1, panel_cols)

    sent, early = half_rows(half_table(0, None))
    own_panel = lax.dynamic_slice_in_dim(panel_blocks, device_id * per_device, per_device, 0)
    own_pos = lax.dynamic_slice_in_dim(panel_pos, device_id * per_device, per_device, 0)
    place = panel_pos % block_count * block_count + panel_pos // block_count
    own_panel, sent = lax.optimization_barrier((own_panel, sent))
    row_part = own_part(
        x_mat, y_inv, own_panel, own_pos, panel_blocks, place.reshape(1, -1), block_count
    )
    early, row_part = lax.optimization_barrier((early, row_part))
    column_part = spread(row_part, "col", cols_size)
    first_slab, first_rows = settle(early)
    table = half_table(1, first_slab)
    column_part, table = lax.optimization_barrier((column_part, table))
    panel_schur = spread(column_part, "row", rows_size)
    sent, late = half_rows(table)

    panel_schur, sent = lax.optimization_barrier((panel_schur, sent))
    symmetric = 0.5 * (panel_schur + panel_schur.T)
    eye = (
        lax.broadcasted_iota(jnp.int32, symmetric.shape, 0)
        == lax.broadcasted_iota(jnp.int32, symmetric.shape, 1)
    )
    diag_shift = 0.01 * jnp.sum(jnp.where(eye, symmetric, 0.0)) / panel_cols
    inverse = inverse_factor(symmetric + jnp.where(eye, diag_shift, 0.0))
    late, inverse = lax.optimization_barrier((late, inverse))
    last_slab, last_rows = settle(late)

    block_rows = trailing.shape[1] // rows_size
    slab = jnp.concatenate([first_slab, last_slab], axis=1)
    head = slab[: block_rows * cols_size].reshape(cols_size, block_rows, panel_cols)
    head = lax.all_to_all(head, "col", split_axis=0, concat_axis=0, tiled=True)[0]
    picked = spread(head, "row", rows_size)

    def halved(matrix):
        rounded = lax.reduce_precision(matrix, exponent_bits=8, mantissa_bits=7)
        low = lax.reduce_precision(matrix - rounded, exponent_bits=8, mantissa_bits=7)
        return rounded.astype(BF16), low.astype(BF16)

    def doubled(matrix):
        return jnp.concatenate(halved(matrix), axis=1)

    high, low = halved(inverse)
    inner = lax.dot_general(
        jnp.concatenate([high, high, low], axis=0), jnp.concatenate([high, low, high], axis=0),
        (((0,), (0,)), ((), ())), preferred_element_type=F32,
    )
    lower_slab = lax.dot_general(
        jnp.concatenate([slab, slab], axis=1), doubled(inverse), (((1,), (1,)), ((), ())),
        preferred_element_type=F32,
    )
    weight = lax.dot_general(
        doubled(inner), jnp.concatenate([picked, picked], axis=1), (((1,), (1,)), ((), ())),
        preferred_element_type=F32,
    )
    weight = doubled(weight.T).T
    return (lower_slab, update([first_rows, last_rows], weight, trailing))


def solution(mesh):
    return jax.shard_map(
        body,
        mesh=mesh,
        in_specs=(
            P(),
            P(),
            P(),
            P(),
            P(),
            P(("row", "col"), None),
            P(("row", "col")),
            P(("row", "col")),
            P(("row", "col")),
            P("row", "col"),
        ),
        out_specs=(P(("row", "col"), None), P("row", "col")),
        check_vma=False,
    )
```

```python
import functools
import math

import jax
import jax.numpy as jnp
from jax import lax
from jax.experimental import pallas as pl
from jax.experimental.pallas import tpu as pltpu
from jax.sharding import PartitionSpec as P


BF16 = jnp.bfloat16
F32 = jnp.float32


def split(value):
    high = value.astype(BF16)
    low = (value - high.astype(F32)).astype(BF16)
    return high, low


def lane_half(rows, width):
    return lax.broadcasted_iota(jnp.int32, (rows, width), 1) < width // 2


def unpack_pairs(panel_ref, pairs, count, block_size):
    lanes = 2 * block_size
    keep = lane_half(count, lanes)
    for c in range(block_size // 2):
        both = panel_ref[:, c * lanes : (c + 1) * lanes].astype(F32)
        turned = pltpu.roll(both, block_size, 1)
        pitch = block_size + 1
        pairs[pl.ds(2 * c, count, stride=pitch), :] = jnp.where(keep, both, turned)
        pairs[pl.ds(2 * c + 1, count, stride=pitch), :] = jnp.where(keep, turned, both)


def column_block(ref, block, slot, block_size):
    lanes = 2 * block_size
    start = pl.multiple_of(block // 2 * lanes, lanes)
    wide = ref[:, pl.ds(start, lanes)]
    return jnp.where(block % 2 == slot, wide, pltpu.roll(wide, block_size, 1))


def group_kernel(block_count, tile, skip, pos_ref, own_ref, x_ref, y_ref, panel_ref, next_ref, out_ref, left, right, pairs, scr, scr_b, mid):
    step = pl.program_id(0)
    order = x_ref.shape[0]
    block_size = order // block_count
    lanes = 2 * block_size
    half = lane_half(order, lanes)

    @pl.when(step == 0)
    def _():
        for s in range(2):
            position = own_ref[s]
            a = pl.multiple_of(position // block_count * block_size, block_size)
            xa = x_ref[pl.ds(a, block_size), :]
            ya = y_ref[pl.ds(a, block_size), :]
            for p in range(block_count):
                cols = slice(p * block_size, (p + 1) * block_size)
                high, low = split(jnp.concatenate([xa[:, cols], ya[:, cols]], axis=1))
                left[p, s * block_size : (s + 1) * block_size, :] = high
                left[p, (2 + s) * block_size : (3 + s) * block_size, :] = low
        for m, ref in enumerate((y_ref, x_ref)):
            first = column_block(ref, own_ref[0] % block_count, 0, block_size)
            second = column_block(ref, own_ref[1] % block_count, 1, block_size)
            high, low = split(jnp.where(half, first, second))
            for q in range(block_count):
                rows = slice(q * block_size, (q + 1) * block_size)
                cols = slice(m * lanes, (m + 1) * lanes)
                right[q, :block_size, cols] = high[rows]
                right[q, block_size:, cols] = low[rows]

    @pl.when(step == 0)
    def _():
        unpack_pairs(panel_ref, pairs, tile, block_size)

    keep = lane_half(block_size, lanes)
    dot = functools.partial(jnp.dot, preferred_element_type=F32)

    def spread(j, e, t):
        position = pos_ref[skip + step * tile + j]
        p = position // block_count
        q = position % block_count
        top = dot(e, right[q])
        low_part = dot(t, right[p])
        for m, part in enumerate((top[:, :lanes], top[:, lanes:], low_part[:, :lanes], low_part[:, lanes:])):
            high, low = split(part)
            rows = slice(m * block_size, (m + 1) * block_size)
            mid[j, rows, :lanes] = high
            mid[j, rows, lanes:] = low

    def two(i, carry):
        pitch = block_size + 1
        block = jnp.concatenate(
            [pairs[pl.ds(2 * i * pitch, block_size), :], pairs[pl.ds((2 * i + 1) * pitch, block_size), :]],
            axis=0,
        )
        turned = block.T[:block_size]
        swapped = pltpu.roll(turned, block_size, 1)
        e = block.astype(BF16)
        spread(2 * i, e[:block_size], jnp.where(keep, turned, swapped).astype(BF16))
        spread(2 * i + 1, e[block_size:], jnp.where(keep, swapped, turned).astype(BF16))
        return carry

    lax.fori_loop(0, tile // 2, two, 0, unroll=tile // 2)

    unpack_pairs(next_ref, pairs, tile, block_size)

    def collect(j, target, row):
        position = pos_ref[skip + step * tile + j]
        a = jnp.concatenate([left[position // block_count], left[position % block_count]], axis=1)
        h = dot(a, mid[j])
        b = block_size
        quad = lambda r, c: jnp.where(
            keep, h[r : r + b, c : c + lanes], h[r + b : r + 2 * b, c : c + lanes]
        )
        target[pl.ds(row * (b + 1), b), :] = quad(0, 0) + (quad(0, lanes) + quad(2 * b, 0))

    part = tile // 2
    keep_t = lane_half(part, lanes)
    for number, target in enumerate((scr, scr_b)):
        for j in range(part):
            collect(number * part + j, target, j)
        rows = slice(number * part, (number + 1) * part)
        for r in range(0, block_size, 2):
            even = target[pl.ds(r, part, stride=block_size + 1), :]
            odd = target[pl.ds(r + 1, part, stride=block_size + 1), :]
            columns = slice(r * block_size, (r + 2) * block_size)
            out_ref[0, rows, columns] = jnp.where(
                keep_t, even, pltpu.roll(odd, block_size, 1)
            ).astype(BF16)
            out_ref[1, rows, columns] = jnp.where(
                keep_t, pltpu.roll(even, block_size, 1), odd
            ).astype(BF16)


def whole(shape):
    return pl.BlockSpec(shape, lambda *_: (0,) * len(shape))


def cost(us, count):
    return pl.CostEstimate(flops=us * 10**9, bytes_accessed=count, transcendentals=0)


def group_table(x, y, panel, positions, own, block_count, part, parts):
    width = panel.shape[1]
    count = panel.shape[0] // parts
    b = x.shape[0] // block_count
    tile = math.gcd(count, 32)
    steps = count // tile
    skip = part * steps
    return pl.pallas_call(
        functools.partial(group_kernel, block_count, tile, part * count),
        grid_spec=pltpu.PrefetchScalarGridSpec(
            num_scalar_prefetch=2,
            grid=(count // tile,),
            in_specs=[
                whole(x.shape),
                whole(y.shape),
                pl.BlockSpec((tile, width), lambda i, *_: (i + skip, 0)),
                pl.BlockSpec((tile, width), lambda i, *_: (jnp.minimum(i + 1, steps - 1) + skip, 0)),
            ],
            out_specs=pl.BlockSpec((2, tile, width), lambda i, *_: (0, i, 0)),
            scratch_shapes=[
                pltpu.VMEM((block_count, 4 * b, 2 * b), BF16),
                pltpu.VMEM((block_count, 2 * b, 4 * b), BF16),
                pltpu.VMEM((tile * (b + 1) + 7, 2 * b), F32),
                pltpu.VMEM((tile // 2 * (b + 1) + 7, 2 * b), F32),
                pltpu.VMEM((tile // 2 * (b + 1) + 7, 2 * b), F32),
                pltpu.VMEM((tile, 4 * b, 4 * b), BF16),
            ],
        ),
        out_shape=jax.ShapeDtypeStruct((2, count, width), BF16),
        cost_estimate=cost(25, 10**7),
        name="group_table",
    )(positions, own, x, y, panel, panel)


def own_kernel(
    block_count, tile, pos_ref, x_ref, y_ref, panel_ref, all_ref, place_ref, out_ref, left, right, pairs, mid, scr, table
):
    step = pl.program_id(0)
    order = x_ref.shape[0]
    b = order // block_count
    lanes = 2 * b
    pitch = b + 1
    positions = block_count * block_count

    @pl.when(step == 0)
    def _():
        for p in range(block_count):
            cols = slice(p * b, (p + 1) * b)
            high, low = split(jnp.concatenate([x_ref[:, cols], y_ref[:, cols]], axis=1))
            left[p, :, :lanes] = high
            left[p, :, lanes:] = low
        for m, ref in enumerate((y_ref, x_ref)):
            for q in range(block_count):
                high, low = split(ref[q * b : (q + 1) * b, :])
                cols = slice(m * order, (m + 1) * order)
                right[q, :b, cols] = high
                right[q, b:, cols] = low
        unpack_pairs(panel_ref, pairs, panel_ref.shape[0], b)

    dot = functools.partial(jnp.dot, preferred_element_type=F32)
    keep = lane_half(block_count, lanes)
    groups = order // lanes
    wide = 2 * lanes

    for j in range(tile):
        position = pos_ref[step * tile + j]
        block = pairs[pl.ds((step * tile + j) * pitch, b), :]
        turned = jnp.concatenate([block, block], axis=0).T[:b]
        top = dot(block.astype(BF16), right[position % block_count])
        low_part = dot(turned.astype(BF16), right[position // block_count])
        parts = (top[:, :order], top[:, order:], low_part[:, :order], low_part[:, order:])
        for m, part in enumerate(parts):
            high, low = split(part)
            mid[j, m * b : (m + 1) * b, :] = high
            mid[j, (4 + m) * b : (5 + m) * b, :] = low
    for j in range(tile):
        position = pos_ref[step * tile + j]
        lp, lq = left[position // block_count], left[position % block_count]
        a = jnp.concatenate([lp[:, :lanes], lq[:, :lanes]], axis=1)
        a_low = jnp.concatenate([lp[:, lanes:], lq[:, lanes:]], axis=1)
        for w in range(order // wide):
            cols = slice(w * wide, (w + 1) * wide)
            high = mid[j, : 4 * b, cols]
            h = dot(jnp.concatenate([a, a_low], axis=1), jnp.concatenate([high, high], axis=0))
            h = h + dot(a, mid[j, 4 * b :, cols])
            for g in range(wide // lanes):
                for i in range(block_count):
                    start = (((j * groups + w * (wide // lanes)) + g) * block_count + i) * pitch
                    scr[start : start + b, :] = h[i * b : (i + 1) * b, g * lanes : (g + 1) * lanes]
    for j in range(tile):
        for g in range(groups):
            base = (j * groups + g) * block_count * pitch
            first = j * positions + 2 * g * block_count
            for r in range(0, b, 2):
                even = scr[pl.ds(base + r, block_count, stride=pitch), :]
                odd = scr[pl.ds(base + r + 1, block_count, stride=pitch), :]
                one = jnp.where(keep, even, pltpu.roll(odd, b, 1))
                two = jnp.where(keep, pltpu.roll(even, b, 1), odd)
                table[first : first + 2 * block_count, r * b : (r + 2) * b] = jnp.concatenate(
                    [one, two], axis=0
                ).astype(BF16)
    products = lax.dot_general(
        table[...], all_ref[...], (((1,), (1,)), ((), ())), preferred_element_type=F32
    )
    hit = (
        lax.broadcasted_iota(jnp.int32, (positions, products.shape[1]), 0) == place_ref[...]
    )
    for j in range(tile):
        part = jnp.where(hit, products[j * positions : (j + 1) * positions], 0.0)
        out_ref[pl.ds(step * tile + j, 1), :] = jnp.sum(part, axis=0, keepdims=True)


def own_part(x, y, panel, positions, everything, place, block_count):
    count, width = panel.shape
    columns = everything.shape[0]
    order = x.shape[0]
    b = order // block_count
    rows = block_count * block_count
    tile = math.gcd(count, 4)
    return pl.pallas_call(
        functools.partial(own_kernel, block_count, tile),
        grid_spec=pltpu.PrefetchScalarGridSpec(
            num_scalar_prefetch=1,
            grid=(count // tile,),
            in_specs=[
                whole(x.shape),
                whole(y.shape),
                whole(panel.shape),
                pl.BlockSpec(everything.shape, lambda *_: (0, 0), pipeline_mode=pl.Buffered(1)),
                whole(place.shape),
            ],
            out_specs=whole((count, columns)),
            scratch_shapes=[
                pltpu.VMEM((block_count, order, 4 * b), BF16),
                pltpu.VMEM((block_count, 2 * b, 2 * order), BF16),
                pltpu.VMEM((max(count, 8) * (b + 1) + 7, 2 * b), F32),
                pltpu.VMEM((tile, 8 * b, order), BF16),
                pltpu.VMEM((tile * order // 2 // b * block_count * (b + 1) + 7, 2 * b), F32),
                pltpu.VMEM((tile * rows, width), BF16),
            ],
        ),
        out_shape=jax.ShapeDtypeStruct((count, columns), F32),
        cost_estimate=cost(22, 10**7),
        name="own_part",
    )(positions, x, y, panel, everything, place)


def row_kernel(cons_ref, table_ref, block_ref, place_ref, out_ref, total):
    step = pl.program_id(0)
    nt = (((1,), (1,)), ((), ()))
    cons = cons_ref[...]
    rows = lax.dot_general(cons, table_ref[0], nt, preferred_element_type=F32)
    block = block_ref[...]
    for s in range(1, table_ref.shape[0]):
        other = lax.dot_general(cons, table_ref[s], nt, preferred_element_type=F32)
        rows = jnp.where(block == s, other, rows)
    rows = rows.astype(BF16)
    places, tile = total.shape[0], cons.shape[0]
    hits = lax.broadcasted_iota(jnp.int32, (places, tile), 0) == place_ref[...]
    part = jnp.dot(jnp.where(hits, 1.0, 0.0).astype(BF16), rows, preferred_element_type=F32)

    @pl.when(step == 0)
    def _():
        total[...] = part

    @pl.when(step > 0)
    def _():
        total[...] += part

    @pl.when(step == pl.num_programs(0) - 1)
    def _():
        out_ref[...] = total[...].astype(BF16)


def send_rows(cons, table, block, place, places):
    slots, width = cons.shape
    cols = table.shape[1]
    tile = math.gcd(slots, 256)
    return pl.pallas_call(
        row_kernel,
        grid=(slots // tile,),
        in_specs=[
            pl.BlockSpec((tile, width), lambda i: (i, 0)),
            pl.BlockSpec(table.shape, lambda i: (0, 0, 0), pipeline_mode=pl.Buffered(1)),
            pl.BlockSpec((tile, 1), lambda i: (i, 0)),
            pl.BlockSpec((1, tile), lambda i: (0, i)),
        ],
        out_specs=whole((places, cols)),
        out_shape=jax.ShapeDtypeStruct((places, cols), BF16),
        scratch_shapes=[pltpu.VMEM((places, cols), F32)],
        cost_estimate=cost(20, 2 * 10**7),
        name="send_rows",
    )(cons, table, block, place)


def update_kernel(parts, *refs):
    row_refs, (weight_ref, trailing_ref, out_ref) = refs[:parts], refs[parts:]
    rows = jnp.concatenate([ref[...] for ref in row_refs] * 2, axis=1)
    out_ref[...] = trailing_ref[...] - jnp.dot(rows, weight_ref[...], preferred_element_type=F32)


def update(row_parts, weight, trailing):
    rows, cols = trailing.shape
    tile = math.gcd(rows, 512)
    return pl.pallas_call(
        functools.partial(update_kernel, len(row_parts)),
        grid=(rows // tile,),
        in_specs=[pl.BlockSpec((tile, part.shape[1]), lambda i: (i, 0)) for part in row_parts]
        + [whole(weight.shape), pl.BlockSpec((tile, cols), lambda i: (i, 0))],
        out_specs=pl.BlockSpec((tile, cols), lambda i: (i, 0)),
        out_shape=jax.ShapeDtypeStruct((rows, cols), F32),
        cost_estimate=cost(8, 2 * 10**7),
        name="update",
    )(*row_parts, weight, trailing)


def hdot(a, b, contract):
    return lax.dot_general(
        a, b, ((contract[:1], contract[1:]), ((), ())),
        precision=lax.Precision.HIGHEST, preferred_element_type=F32,
    )


def factor_kernel(block, s_ref, out_ref, a):
    order = s_ref.shape[0]
    count = order // block
    groups = block // 8
    a[...] = s_ref[...]
    row_id = lax.broadcasted_iota(jnp.int32, (8, 1), 0)
    eye = (
        lax.broadcasted_iota(jnp.int32, (block, block), 0)
        == lax.broadcasted_iota(jnp.int32, (block, block), 1)
    ).astype(F32)

    def diagonal(b, carry):
        start = pl.multiple_of(b * block, block)
        tile = (8, block)
        left = [a[pl.ds(start + 8 * g, 8), pl.ds(start, block)] for g in range(groups)]
        right = [eye[8 * g : 8 * g + 8, :] for g in range(groups)]
        for g in range(groups):
            spot = lambda i, s, t: jnp.broadcast_to(
                left[i][s : s + 1, 8 * g + t : 8 * g + t + 1], tile
            )
            d = {(s, t): spot(g, s, t) for t in range(8) for s in range(t, 8)}
            inv, low, scaled = [], {}, []
            heads = [
                [jnp.broadcast_to(side[g][t : t + 1, :], tile) for side in (left, right)]
                for t in range(8)
            ]
            for t in range(8):
                root = lax.rsqrt(d[t, t])
                root = root * (1.5 - 0.5 * d[t, t] * root * root)
                inv.append(root)
                for s in range(t + 1, 8):
                    low[s, t] = d[s, t] * root
                for u in range(t + 1, 8):
                    for s in range(u, 8):
                        d[s, u] = d[s, u] - low[s, t] * low[u, t]
                now = heads[t]
                for u in range(t):
                    now = [n - low[t, u] * r for n, r in zip(now, scaled[u])]
                scaled.append([n * root for n in now])
            for i in range(g + 1, groups):
                mult = []
                for t in range(8):
                    m = jnp.broadcast_to(left[i][:, 8 * g + t : 8 * g + t + 1], tile)
                    for u in range(t):
                        m = m - mult[u] * low[t, u]
                    mult.append(m * inv[t])
                for t in range(8):
                    left[i] = left[i] - mult[t] * scaled[t][0]
                    right[i] = right[i] - mult[t] * scaled[t][1]
            done = scaled[0][1]
            for t in range(1, 8):
                done = jnp.where(row_id == t, scaled[t][1], done)
            right[g] = done
        inverse = jnp.concatenate(right, axis=0)
        out_ref[pl.ds(start, block), pl.ds(start, block)] = inverse
        panel = hdot(a[:, pl.ds(start, block)], inverse, (1, 1))
        below = lax.broadcasted_iota(jnp.int32, (order, 1), 0) >= start + block
        panel = jnp.where(below, panel, 0.0)
        a[:, pl.ds(start, block)] = panel
        return carry, panel

    def body(b, carry):
        _, panel = diagonal(b, carry)
        start = pl.multiple_of(b * block, block)

        for i in range(1, count):
            @pl.when(b < i)
            def _():
                piece = a[i * block : (i + 1) * block, pl.ds(start, block)]
                cols = slice(i * block, (i + 1) * block)
                a[:, cols] = a[:, cols] - hdot(panel, piece, (1, 1))

        return carry

    lax.fori_loop(0, count, body, 0)
    for i in range(count):
        for b in range(i + 1, count):
            out_ref[i * block : (i + 1) * block, b * block : (b + 1) * block] = jnp.zeros(
                (block, block), F32
            )
    for i in range(1, count):
        low_row = a[i * block : (i + 1) * block, : i * block]
        total = hdot(low_row, out_ref[: i * block, : i * block], (1, 0))
        own = out_ref[i * block : (i + 1) * block, i * block : (i + 1) * block]
        out_ref[i * block : (i + 1) * block, : i * block] = -hdot(own, total, (1, 0))


def inverse_factor(matrix):
    order = matrix.shape[0]
    block = 128
    return pl.pallas_call(
        functools.partial(factor_kernel, block),
        in_specs=[pl.BlockSpec(memory_space=pltpu.VMEM)],
        out_specs=pl.BlockSpec(memory_space=pltpu.VMEM),
        out_shape=jax.ShapeDtypeStruct((order, order), F32),
        scratch_shapes=[pltpu.VMEM((order, order), F32)],
        cost_estimate=cost(30, 10**6),
        name="inverse_factor",
    )(matrix)


def body(
    x_mat,
    y_inv,
    panel_blocks,
    panel_pos,
    group_blocks,
    cons_blocks,
    slot_block,
    slot_row,
    group_size,
    trailing,
):
    rows_size = lax.axis_size("row")
    cols_size = lax.axis_size("col")
    devices = rows_size * cols_size
    col_index = lax.axis_index("col")
    device_id = lax.axis_index("row") * cols_size + col_index
    panel_cols = panel_blocks.shape[0]
    per_device = panel_cols // devices
    order = x_mat.shape[0]
    block_size = math.isqrt(panel_blocks.shape[1])
    block_count = order // block_size
    slot_count = cons_blocks.shape[0]

    sub_rows = trailing.shape[0] // cols_size
    base_share = sub_rows // devices
    spread = sub_rows - devices // 4 * base_share
    capacity = base_share + (spread + devices - 1) // devices
    places = devices * capacity
    slot_ids = jnp.arange(slot_count, dtype=jnp.int32)
    live_slots = slot_ids < group_size[0]
    target = slot_row // sub_rows
    dest_hits = (
        target[:, None] == jnp.arange(devices, dtype=jnp.int32)[None, :]
    ) & live_slots[:, None]
    earlier = (slot_ids[:, None] > slot_ids[None, :]).astype(BF16)
    before = jnp.dot(earlier, dest_hits.astype(BF16), preferred_element_type=F32)
    dest_rank = jnp.sum(jnp.where(dest_hits, before, 0.0), axis=1).astype(jnp.int32)
    slot_place = jnp.where(live_slots, target * capacity + dest_rank, places)
    exchange = functools.partial(
        lax.all_to_all, axis_name=("row", "col"), split_axis=0, concat_axis=0, tiled=True
    )

    own_group = lax.dynamic_index_in_dim(group_blocks, device_id, 0, keepdims=False)
    block_column, place_row = slot_block.reshape(-1, 1), slot_place.reshape(1, -1)
    halves = 2
    width = panel_cols // halves

    def half_table(half, after):
        x_now = x_mat if after is None else lax.optimization_barrier((x_mat, after))[0]
        return group_table(
            x_now, y_inv, panel_blocks, panel_pos, own_group, block_count, half, halves
        )

    def half_rows(table, ahead):
        sent = send_rows(cons_blocks, table, block_column, place_row, places)
        sent, ahead = lax.optimization_barrier((sent, ahead))
        return ahead, sent, exchange(sent.reshape(devices, capacity, width))

    def settle(rows):
        slab = jnp.dot(recv_hits, rows.reshape(-1, width), preferred_element_type=F32).astype(BF16)
        return slab, lax.all_gather(slab, "col", axis=0, tiled=True)

    place_ids = jnp.arange(places, dtype=jnp.int32)
    tag = slot_row % sub_rows + 1
    arriving = place_ids[:, None] == slot_place[None, :]
    send_local = jnp.sum(jnp.where(arriving, tag[None, :], 0), axis=1).astype(F32) - 1.0
    padded = jnp.pad(send_local, (0, 16 * panel_cols - places)).reshape(16, panel_cols)
    tags = lax.all_gather(padded, ("row", "col"), axis=0, tiled=True)
    recv_local = lax.dynamic_index_in_dim(
        tags.reshape(devices, -1)[:, :places].reshape(devices, devices, capacity),
        device_id, 1, keepdims=False,
    ).astype(jnp.int32)
    local_ids = jnp.arange(sub_rows, dtype=jnp.int32)
    recv_hits = (local_ids[:, None] == recv_local.reshape(1, -1)).astype(BF16)

    def spread(part, axis, size):
        copies = jnp.broadcast_to(part[None], (size,) + part.shape)
        copies = lax.all_to_all(copies, axis, split_axis=0, concat_axis=0, tiled=True)
        return copies.reshape(-1, panel_cols)

    _, sent, early = half_rows(half_table(0, None), slot_place)
    own_panel = lax.dynamic_slice_in_dim(panel_blocks, device_id * per_device, per_device, 0)
    own_pos = lax.dynamic_slice_in_dim(panel_pos, device_id * per_device, per_device, 0)
    place = panel_pos % block_count * block_count + panel_pos // block_count
    own_panel, sent = lax.optimization_barrier((own_panel, sent))
    row_part = own_part(
        x_mat, y_inv, own_panel, own_pos, panel_blocks, place.reshape(1, -1), block_count
    )
    early, row_part = lax.optimization_barrier((early, row_part))
    column_part = spread(row_part, "col", cols_size)
    first_slab, first_rows = settle(early)
    table = half_table(1, first_slab)
    column_part, table = lax.optimization_barrier((column_part, table))
    panel_schur = spread(column_part, "row", rows_size)
    panel_schur, sent, late = half_rows(table, panel_schur)

    panel_schur, sent = lax.optimization_barrier((panel_schur, sent))
    symmetric = 0.5 * (panel_schur + panel_schur.T)
    eye = (
        lax.broadcasted_iota(jnp.int32, symmetric.shape, 0)
        == lax.broadcasted_iota(jnp.int32, symmetric.shape, 1)
    )
    diag_shift = 0.01 * jnp.sum(jnp.where(eye, symmetric, 0.0)) / panel_cols
    shifted = symmetric + jnp.where(eye, diag_shift, 0.0)
    last_slab, last_rows = settle(late)
    shifted, last_slab = lax.optimization_barrier((shifted, last_slab))
    inverse = inverse_factor(shifted)

    block_rows = trailing.shape[1] // rows_size
    slab = jnp.concatenate([first_slab, last_slab], axis=1)
    head = slab[: block_rows * cols_size].reshape(cols_size, block_rows, panel_cols)
    head = lax.all_to_all(head, "col", split_axis=0, concat_axis=0, tiled=True)[0]
    picked = spread(head, "row", rows_size)

    def halved(matrix):
        rounded = lax.reduce_precision(matrix, exponent_bits=8, mantissa_bits=7)
        low = lax.reduce_precision(matrix - rounded, exponent_bits=8, mantissa_bits=7)
        return rounded.astype(BF16), low.astype(BF16)

    def doubled(matrix):
        return jnp.concatenate(halved(matrix), axis=1)

    high, low = halved(inverse)
    inner = lax.dot_general(
        jnp.concatenate([high, high, low], axis=0), jnp.concatenate([high, low, high], axis=0),
        (((0,), (0,)), ((), ())), preferred_element_type=F32,
    )
    lower_slab = lax.dot_general(
        jnp.concatenate([slab, slab], axis=1), doubled(inverse), (((1,), (1,)), ((), ())),
        preferred_element_type=F32,
    )
    weight = lax.dot_general(
        doubled(inner), jnp.concatenate([picked, picked], axis=1), (((1,), (1,)), ((), ())),
        preferred_element_type=F32,
    )
    weight = doubled(weight.T).T
    return (lower_slab, update([first_rows, last_rows], weight, trailing))


def solution(mesh):
    return jax.shard_map(
        body,
        mesh=mesh,
        in_specs=(
            P(),
            P(),
            P(),
            P(),
            P(),
            P(("row", "col"), None),
            P(("row", "col")),
            P(("row", "col")),
            P(("row", "col")),
            P("row", "col"),
        ),
        out_specs=(P(("row", "col"), None), P("row", "col")),
        check_vma=False,
    )
```
